512 devices in a mesh: head: 8 (over y), ctx: 16 (over z, core), rep: 4 (over x).
Axes of the slice: x: 4, y: 8, z: 8, core: 2. Of those that a mesh axis runs over, the one named last changes fastest.
Arguments:
- inputs: bfloat16 [4, 8192, 8192], P('rep', 'ctx', 'head'), may hold values from -6 to 6
- b_proj: bfloat16 [4, 8192, 2048], P('rep', 'ctx', 'head'), may hold values from -0.375 to 0.375
- c_proj: bfloat16 [4, 8192, 2048], P('rep', 'ctx', 'head'), may hold values from -0.375 to 0.375
- log_decay: bfloat16 [4, 128, 8192], P('rep', 'head', 'ctx'), may hold values from -1 to 0
- starts: int32 [4, 8192], P('rep', 'ctx'), may hold values 0 or 1
- counts: int32 [4, 16], P('rep', 'ctx'), may hold values from 0 to 512, as said below
- skip_gain: float32 [128], P('head'), may hold values from 0.5 to 1.5
- readout: bfloat16 [8192], P('head'), may hold values from -0.0625 to 0.0625
Outputs:
- ssd_out: bfloat16 [4, 8192, 8192], P('rep', 'ctx', 'head')
- token_scores: float32 [4, 8192], P('rep', 'ctx')
The draws below stay inside these ranges and needn't reach their ends.
Inputs may be any that keep to these rules, and one draw needn't show every extreme that they name: `counts`: at each ctx index, the two rows 2q and 2q + 1 (q = 0, 1, ...) together hold live slots in exactly 2 spans, counting ceil(count / 256) for each; one of the two holds all of them and the other none.
All inputs are finite; a program needn't handle non-finite values. No bound on the sum of `starts` on one device may be relied on, other than what follows from the above.
Results may differ from the reference program's by a relative error of at most 0.0056.
Values may be sent and summed in bfloat16 or wider, within the bound.
A program may use at most 64 MiB of HBM per device.

```python
import math
import jax
import jax.numpy as jnp
from jax import lax

HEAD_DIM = 64
STATE = 256
SPAN = 256
SPANS_DEV = 2
HEAD_TOTAL = 128
GROUPS = 8
TOK_DEV = 512
TOKEN_SLOTS = 8192
PACKED_ROWS = 4
CTXS = 16


def draw_log_decay(key, part):
    random_subkeys = jax.random.split(key, 7)
    device_count = TOKEN_SLOTS // TOK_DEV
    fast_share = 0.5
    is_fast = jax.random.uniform(random_subkeys[0], (PACKED_ROWS, HEAD_TOTAL)) < fast_share
    slow_rate = jax.random.uniform(random_subkeys[1], (PACKED_ROWS, HEAD_TOTAL), minval=0.15, maxval=0.5) / TOKEN_SLOTS
    fast_rate = 1.0 / jax.random.uniform(random_subkeys[2], (PACKED_ROWS, HEAD_TOTAL), minval=30.0, maxval=50.0)
    base_rate = jnp.where(is_fast, fast_rate, slow_rate)
    device_factor = jnp.exp(jax.random.uniform(random_subkeys[3], (PACKED_ROWS, HEAD_TOTAL, device_count), minval=math.log(0.5), maxval=math.log(1.5)))
    device_factor = jnp.repeat(device_factor, TOK_DEV, axis=2)
    roughness = jax.random.uniform(random_subkeys[4], (PACKED_ROWS, HEAD_TOTAL, TOKEN_SLOTS), minval=0.6, maxval=1.4)
    logarithm_rate = -base_rate[:, :, None] * device_factor * roughness
    spike_position = jax.random.randint(random_subkeys[5], (PACKED_ROWS, 2), 0, TOKEN_SLOTS)
    spike_penalty = jax.random.uniform(random_subkeys[6], (PACKED_ROWS, HEAD_TOTAL, 2), minval=0.2, maxval=0.5)
    reset_positions = jnp.arange(TOKEN_SLOTS)
    for chosen_index in range(2):
        reset_flags = reset_positions[None, :] == spike_position[:, chosen_index:chosen_index + 1]
        logarithm_rate = logarithm_rate + jnp.where(reset_flags[:, None, :], jnp.log(1.0 - spike_penalty[:, :, chosen_index])[:, :, None], 0.0)
    return logarithm_rate.astype(jnp.bfloat16)


def draw_counts(key, part):
    random_subkeys = jax.random.split(key, 2)
    pair_count = PACKED_ROWS // 2
    lower_full = jax.random.randint(random_subkeys[0], (CTXS, pair_count), 0, 2)
    full_flags = jnp.stack([lower_full, 1 - lower_full], axis=2).reshape(CTXS, PACKED_ROWS)
    tail_sizes = jax.random.randint(random_subkeys[1], (CTXS, PACKED_ROWS), 1, SPAN + 1)
    tail_sizes = jnp.where(jnp.arange(CTXS)[:, None] == 0, SPAN, tail_sizes)
    filled = full_flags * ((SPANS_DEV - 1) * SPAN + tail_sizes)
    return filled.T.astype(jnp.int32)


def set_ends(result, stream_key, low, largest):
    longest = result.shape.index(max(result.shape))
    spots = []
    for shift in (0, 1):
        where = [jax.random.randint(jax.random.fold_in(stream_key, axis), (), 0, length) for axis, length in enumerate(result.shape)]
        where[longest] = (where[longest] + shift) % result.shape[longest]
        spots.append(tuple(where))
    return result.at[spots[0]].set(low).at[spots[1]].set(largest)


def steps_of(rng, extent, shards, least, top_value):
    loudness = 1.0
    for dim, blocks in shards:
        draws = jax.random.uniform(jax.random.fold_in(jax.random.fold_in(rng, 6), dim), (blocks,), jnp.float32, least / len(shards), top_value / len(shards))
        loudness = loudness * jnp.repeat(jnp.exp(draws), extent[dim] // blocks).reshape((-1,) + (1,) * (len(extent) - 1 - dim))
    return loudness


def noise(stream_key, shape, scale, bound, cuts=(), kind=jnp.bfloat16):
    values = jax.random.normal(stream_key, shape, jnp.float32) * scale
    if len(cuts) > 0:
        values = steps_of(stream_key, shape, cuts, -0.22, 0.18) * values
    return jnp.clip(values, min=-bound, max=bound).astype(kind)


def setup_inputs(seed: int = 0) -> dict:
    keys = jax.random.split(jax.random.key(seed), 9)
    inputs = noise(keys[0], (PACKED_ROWS, TOKEN_SLOTS, HEAD_TOTAL * HEAD_DIM), 1.0, 6.0, ((0, 4), (1, 16), (2, 8)))
    b_proj = noise(keys[1], (PACKED_ROWS, TOKEN_SLOTS, GROUPS * STATE), 0.0625, 0.375, ((0, 4), (1, 16), (2, 8)))
    c_proj = noise(keys[2], (PACKED_ROWS, TOKEN_SLOTS, GROUPS * STATE), 0.0625, 0.375, ((0, 4), (1, 16), (2, 8)))
    log_decay = draw_log_decay(jax.random.fold_in(keys[8], 71), 0)
    starts = set_ends((jax.random.randint(keys[4], (PACKED_ROWS, TOKEN_SLOTS), 0, TOKEN_SLOTS) < 3).astype(jnp.int32), jax.random.fold_in(keys[4], 1), 0, 1)
    counts = draw_counts(jax.random.fold_in(keys[8], 71), 0)
    skip_gain = jnp.clip(0.5 + 1.0 * jax.random.uniform(keys[6], (HEAD_TOTAL,), jnp.float32) ** steps_of(keys[6], (HEAD_TOTAL,), ((0, 8),), -0.2, 0.2), 0.5, 1.5)
    readout = noise(keys[7], (HEAD_TOTAL * HEAD_DIM,), (HEAD_TOTAL * HEAD_DIM) ** -0.5, 0.0625, ((0, 8),))
    return dict(inputs=inputs, b_proj=b_proj, c_proj=c_proj, log_decay=log_decay, starts=starts, counts=counts, skip_gain=skip_gain, readout=readout)


precise = lax.Precision.HIGHEST


def span_terms(span_x, span_b, span_c, span_a, span_s):
    length = span_x.shape[0]
    reset_positions = jnp.arange(length)
    triangle = (reset_positions[:, None] <= reset_positions[None, :]).astype(jnp.float32)
    cum_decay = jnp.einsum('gkj,ji->gki', span_a, triangle, precision=precise)
    doc_index = jnp.dot(span_s.astype(jnp.float32), triangle, precision=precise)
    causal = reset_positions[:, None] >= reset_positions[None, :]
    same_doc = causal & (doc_index[:, None] == doc_index[None, :])
    decay_gaps = cum_decay[..., :, None] - cum_decay[..., None, :]
    decay_mat = jnp.where(same_doc, jnp.exp(jnp.minimum(decay_gaps, 0.0)), 0.0)
    scores = jnp.einsum('ign,jgn->gij', span_c.astype(jnp.float32), span_b.astype(jnp.float32))
    weights = (decay_mat * scores[:, None]).astype(jnp.bfloat16)
    diag_out = jnp.einsum('gkij,jgkp->igkp', weights.astype(jnp.float32), span_x.astype(jnp.float32)).astype(jnp.bfloat16)
    last_cum = cum_decay[..., -1]
    end_keep = jnp.where(doc_index == doc_index[-1], jnp.exp(last_cum[..., None] - cum_decay), 0.0)
    b_groups = jnp.transpose(span_b, (1, 0, 2))[:, None].astype(jnp.float32)
    weighted_b = (end_keep[..., None] * b_groups).astype(jnp.bfloat16)
    span_state = jnp.einsum('gkjn,jgkp->gkpn', weighted_b.astype(jnp.float32), span_x.astype(jnp.float32))
    span_total = jnp.where(doc_index[-1] == 0, jnp.exp(last_cum), 0.0)
    entry_keep = jnp.where(doc_index == 0, jnp.exp(cum_decay), 0.0)
    return diag_out, span_state, span_total, entry_keep


def reference(inputs, b_proj, c_proj, log_decay, starts, counts, skip_gain, readout):
    groups = GROUPS
    per_group = HEAD_TOTAL // GROUPS
    positions = jnp.arange(TOKEN_SLOTS)
    live_mask = (positions % TOK_DEV)[None, :] < counts[:, positions // TOK_DEV]
    masked_x = jnp.where(live_mask[..., None], inputs, jnp.zeros((), inputs.dtype))
    masked_a = jnp.where(live_mask[:, None, :], log_decay.astype(jnp.float32), 0.0)
    masked_s = jnp.where(live_mask, starts, 0)
    blocks = TOKEN_SLOTS // SPAN
    x_blocks = masked_x.reshape(PACKED_ROWS, blocks, SPAN, groups, per_group, HEAD_DIM)
    b_blocks = b_proj.reshape(PACKED_ROWS, blocks, SPAN, groups, STATE)
    c_blocks = c_proj.reshape(PACKED_ROWS, blocks, SPAN, groups, STATE)
    a_blocks = masked_a.reshape(PACKED_ROWS, groups, per_group, blocks, SPAN).transpose(0, 3, 1, 2, 4)
    s_blocks = masked_s.reshape(PACKED_ROWS, blocks, SPAN)
    l_blocks = live_mask.reshape(PACKED_ROWS, blocks, SPAN).astype(jnp.float32)
    skip_rows = skip_gain.reshape(groups, per_group)

    def advance(carried, span_items):
        span_x, span_b, span_c, span_a, span_s, span_l = span_items
        diag_out, span_state, span_total, entry_keep = span_terms(span_x, span_b, span_c, span_a, span_s)
        entering = carried.astype(jnp.bfloat16)
        off_out = jnp.einsum('ign,gkpn->igkp', span_c.astype(jnp.float32), entering.astype(jnp.float32))
        mixed_out = diag_out.astype(jnp.float32) + off_out * jnp.transpose(entry_keep, (2, 0, 1))[..., None]
        mixed_out = mixed_out + skip_rows[None, :, :, None] * span_x.astype(jnp.float32)
        mixed_out = (mixed_out * span_l[:, None, None, None]).astype(jnp.bfloat16)
        carried = span_total[..., None, None] * carried + span_state
        return carried, mixed_out

    def one_row(row_items):
        zero_state = jnp.zeros((groups, per_group, HEAD_DIM, STATE), jnp.float32)
        return lax.scan(advance, zero_state, row_items)[1]

    mixed_all = lax.map(one_row, (x_blocks, b_blocks, c_blocks, a_blocks, s_blocks, l_blocks))
    ssd_out = mixed_all.reshape(PACKED_ROWS, TOKEN_SLOTS, HEAD_TOTAL * HEAD_DIM)
    token_scores = jnp.dot(ssd_out.reshape(PACKED_ROWS * TOKEN_SLOTS, HEAD_TOTAL * HEAD_DIM), readout, preferred_element_type=jnp.float32)
    return ssd_out, token_scores.reshape(PACKED_ROWS, TOKEN_SLOTS)
```

```python
import functools
import math

import jax
import jax.numpy as jnp
from jax import lax
from jax.experimental import pallas as pl
from jax.experimental.pallas import tpu as pltpu
from jax.sharding import PartitionSpec as P

SPAN = 256
HALF = 128
SUB = 64
LANES = 128
ROWS_STEP = 128
LOG2E = math.log2(math.e)
F32 = jnp.float32
BF16 = jnp.bfloat16
MESH = pl.DeviceIdType.MESH


def mm(a, b):
    return lax.dot_general(a, b, (((1,), (0,)), ((), ())), preferred_element_type=F32)


def mm_nt(a, b):
    return lax.dot_general(a, b, (((1,), (1,)), ((), ())), preferred_element_type=F32)


def mm_tn(a, b):
    return lax.dot_general(a, b, (((0,), (0,)), ((), ())), preferred_element_type=F32)


def iota(shape, dim):
    return lax.broadcasted_iota(jnp.int32, shape, dim)


def kernel(
    sizes,
    count_ref, x_ref, b_ref, c_ref, a_ref, s_ref, gain_ref, read_ref,
    out_ref, score_ref,
    xm, lx, cum, doc, bt, first, whole, ta, td, sbf, srecv, trecv,
    comb, tcomb, base, tbase, ein, snd, eown, psnd, y, gb, gm, sums,
    psem_s, psem_r, tsem, csem_s, csem_r, fsem_s, fsem_r, ysem_s, ysem_r,
):
    ctxs, heads_axis, tokens, tiles = sizes
    half = tiles // 2
    spans = tokens // SPAN
    steps = SPAN // ROWS_STEP
    last_chip = ctxs // 2 - 1
    ctx = lax.axis_index("ctx")
    core = lax.rem(ctx, 2)
    chip = ctx // 2
    mine = lax.axis_index("head")
    partner = ctx + 1 - 2 * core
    follow = lax.rem(ctx + 2, ctxs)
    before = lax.rem(ctx + ctxs - 2, ctxs)

    barrier = pltpu.get_barrier_semaphore()
    for other in (partner, follow, before):
        pl.semaphore_signal(barrier, inc=1, device_id={"ctx": other}, device_id_type=MESH)
    for k in range(1, heads_axis):
        pl.semaphore_signal(
            barrier, inc=1, device_id={"head": lax.rem(mine + k, heads_axis)}, device_id_type=MESH
        )

    count = count_ref[0, 0]
    live_row = iota((1, tokens), 1) < count
    log_decay = jnp.where(live_row, a_ref[0].astype(F32), 0.0).astype(BF16)
    starts = jnp.where(live_row, s_ref[...].astype(F32), 0.0)
    head_rows = log_decay.shape[0]
    starts = jnp.where(iota((head_rows, tokens), 0) == 0, starts, 0.0).astype(BF16)
    spread = (iota((head_rows, tiles * LANES), 0) == iota((head_rows, tiles * LANES), 1) // SUB)
    spread = jnp.where(spread, 1.0, 0.0).astype(BF16)
    ones = jnp.ones((head_rows, LANES), BF16)
    tri = jnp.where(iota((SPAN, SPAN), 0) >= iota((SPAN, SPAN), 1), 1.0, 0.0).astype(BF16)
    for s in range(spans):
        rows = pl.ds(s * SPAN, SPAN)
        lx[rows, :] = mm_tn(log_decay[:, s * SPAN : (s + 1) * SPAN], spread).astype(BF16)
        spread_starts = mm_tn(starts[:, s * SPAN : (s + 1) * SPAN], ones).astype(BF16)
        doc[rows, :] = mm(tri, spread_starts)
        bt[:, rows] = b_ref[0, rows, :].astype(F32).T.astype(BF16)

    live = iota((tokens, LANES), 0) < count

    def state_tile(t):
        cols = pl.ds(pl.multiple_of(t * LANES, LANES), LANES)
        xt = jnp.where(live, x_ref[0, :, cols].astype(F32), 0.0).astype(BF16)
        xm[t] = xt
        states, totals = [], []
        for s in range(spans):
            rows = slice(s * SPAN, (s + 1) * SPAN)
            run = mm(tri, lx[pl.ds(s * SPAN, SPAN), cols]) * LOG2E
            cum[t, pl.ds(s * SPAN, SPAN), :] = run
            docs = doc[pl.ds(s * SPAN, SPAN), :]
            last = run[SPAN - 1 : SPAN, :]
            keep = jnp.where(docs == docs[SPAN - 1 : SPAN, :], jnp.exp2(last - run), 0.0)
            weighted = (xt[rows, :].astype(F32) * keep).astype(BF16)
            states.append(mm(bt[:, pl.ds(s * SPAN, SPAN)], weighted))
            totals.append(jnp.where(docs[SPAN - 1 : SPAN, :] == 0.0, jnp.exp2(last), 0.0))
        first[t] = states[0]
        joined = totals[1] * states[0] + states[1]
        whole[t] = joined
        ta[t] = jnp.broadcast_to(totals[0], (8, LANES))
        td[t] = jnp.broadcast_to(totals[0] * totals[1], (8, LANES))
        return joined

    for j in range(half):
        sbf[j] = state_tile((1 - core) * half + j).astype(BF16)
        if j == 0:
            pl.semaphore_wait(barrier, 3 + heads_axis - 1)
        state_copy(sbf, srecv, psem_s, psem_r, j, partner).start()
    t_copy = pltpu.make_async_remote_copy(
        src_ref=td.at[pl.ds((1 - core) * half, half)],
        dst_ref=trecv,
        send_sem=tsem.at[0],
        recv_sem=tsem.at[1],
        device_id={"ctx": partner},
        device_id_type=MESH,
    )
    t_copy.start()
    for j in range(half):
        state_tile(core * half + j)

    t_copy.wait_recv()
    for j in range(half):
        state_copy(sbf, srecv, psem_s, psem_r, j, partner).wait_recv()
        own, theirs = whole[core * half + j], srecv[j].astype(F32)
        t_own, t_theirs = td[core * half + j], trecv[j]
        is_low = core == 0
        low, high = jnp.where(is_low, own, theirs), jnp.where(is_low, theirs, own)
        t_low, t_high = jnp.where(is_low, t_own, t_theirs), jnp.where(is_low, t_theirs, t_own)
        comb[j] = t_high[0:1, :] * low + high
        tcomb[j] = t_high * t_low
        base[j] = low
        tbase[j] = t_low

    def chain_copy(j, r):
        piece = pl.ds(r * ROWS_STEP, ROWS_STEP)
        return pltpu.make_async_remote_copy(
            src_ref=snd.at[j, piece],
            dst_ref=ein.at[j, piece],
            send_sem=csem_s.at[j, r],
            recv_sem=csem_r.at[j, r],
            device_id={"ctx": follow},
            device_id_type=MESH,
        )

    def pass_copy(j, r):
        piece = pl.ds(r * ROWS_STEP, ROWS_STEP)
        return pltpu.make_async_remote_copy(
            src_ref=psnd.at[j, piece],
            dst_ref=eown.at[core * half + j, piece],
            send_sem=fsem_s.at[j, r],
            recv_sem=fsem_r.at[j, r],
            device_id={"ctx": partner},
            device_id_type=MESH,
        )

    def local_part():
        for s in range(spans):
            rows = pl.ds(s * SPAN, SPAN)
            scores = mm_nt(c_ref[0, rows, :], b_ref[0, rows, :])
            gb[s] = scores.astype(BF16)
        lane = iota((SUB, LANES), 1)
        lane = jnp.where(lane < SUB, lane, lane - SUB)
        row = iota((SUB, LANES), 0)
        eye = jnp.where(row == lane, 1.0, 0.0)
        for k in range(tokens // SUB):
            rows = pl.ds(k * SUB, SUB)
            bk = b_ref[0, rows, :]
            sc = mm_nt(c_ref[0, rows, :], jnp.concatenate([bk, bk], axis=0))
            dk = doc[rows, :]
            drow = jnp.sum(dk * eye, axis=0, keepdims=True)
            gm[k] = jnp.where((row >= lane) & (dk == drow), sc, 0.0)
        low_lane = iota((SUB, LANES), 1) < SUB
        one_lane = iota((1, LANES), 1) < SUB

        def tile(t, _):
            skip = jnp.where(one_lane, gain_ref[2 * t], gain_ref[2 * t + 1])
            for s in range(spans):
                o = s * SPAN

                def level(at, width):
                    lo, hi = pl.ds(o + at, width), pl.ds(o + at + width, width)
                    run_lo, run_hi = cum[t, lo, :], cum[t, hi, :]
                    doc_lo, doc_hi = doc[lo, :], doc[hi, :]
                    ref, ref_doc = run_lo[width - 1 : width, :], doc_lo[width - 1 : width, :]
                    keep = jnp.where(doc_lo == ref_doc, jnp.exp2(ref - run_lo), 0.0)
                    enter = jnp.where(doc_hi == ref_doc, jnp.exp2(run_hi - ref), 0.0)
                    weighted = (xm[t, lo, :].astype(F32) * keep).astype(BF16)
                    part = gb[s, at + width : at + 2 * width, at : at + width]
                    return enter * mm(part, weighted)

                far = level(0, HALF)
                near = [level(0, SUB), level(HALF, SUB)]
                for q in range(SPAN // SUB):
                    rows = pl.ds(o + q * SUB, SUB)
                    run = cum[t, rows, :]
                    xq = xm[t, rows, :]
                    xf = xq.astype(F32)
                    run_row = jnp.sum(run * eye, axis=0, keepdims=True)
                    w = jnp.exp2(jnp.minimum(run - run_row, 0.0)) * gm[s * (SPAN // SUB) + q]
                    left = jnp.where(low_lane, xf, 0.0).astype(BF16)
                    right = jnp.where(low_lane, 0.0, xf).astype(BF16)
                    v = mm(w.astype(BF16), jnp.concatenate([left, right], axis=0))
                    v = v + skip * xf
                    if q % 2 == 1:
                        v = v + near[q // 2]
                    if q >= 2:
                        v = v + far[(q - 2) * SUB : (q - 1) * SUB, :]
                    y[t, rows, :] = v
            return 0

        lax.fori_loop(0, tiles, tile, 0)

    early = chip < (last_chip + 1) // 2
    pl.when(jnp.logical_not(early))(local_part)

    @pl.when(chip == 0)
    def _():
        ein[...] = jnp.zeros_like(ein)

    for j in range(half):
        for r in range(steps):
            piece = pl.ds(r * ROWS_STEP, ROWS_STEP)
            pl.when(chip > 0)(lambda: chain_copy(j, r).wait_recv())
            e16 = ein[j, piece, :]
            e = e16.astype(F32)

            @pl.when(chip < last_chip)
            def _():
                snd[j, piece, :] = (tcomb[j, 0:1, :] * e + comb[j, piece, :]).astype(BF16)
                chain_copy(j, r).start()

            f = tbase[j, 0:1, :] * e + base[j, piece, :]
            eown[core * half + j, piece, :] = jnp.where(core == 0, e, f).astype(BF16)
            psnd[j, piece, :] = jnp.where(core == 0, f, e).astype(BF16)
            pass_copy(j, r).start()

    pl.when(early)(local_part)

    row_scores = jnp.zeros((8, tokens), F32)

    def finish_tile(t, row_scores):
        cols = pl.ds(pl.multiple_of(t * LANES, LANES), LANES)
        e0 = eown[t]
        e1 = (ta[t][0:1, :] * e0.astype(F32) + first[t]).astype(BF16)
        parts = []
        for s, e in enumerate((e0, e1)):
            rows = pl.ds(s * SPAN, SPAN)
            enter = jnp.where(doc[rows, :] == 0.0, jnp.exp2(cum[t, rows, :]), 0.0)
            v = y[t, rows, :] + enter * mm(c_ref[0, rows, :], e)
            v = jnp.where(live[s * SPAN : (s + 1) * SPAN, :], v, 0.0).astype(BF16)
            out_ref[0, rows, cols] = v
            parts.append(v)
        v = jnp.concatenate(parts, axis=0)
        weight = jnp.broadcast_to(read_ref[:, cols].astype(F32), (16, LANES)).astype(BF16)
        return row_scores + mm_nt(weight, v)[0:8, :]

    for j in range(half):
        row_scores = finish_tile(core * half + j, row_scores)
    for j in range(half):
        for r in range(steps):
            piece = pl.ds(r * ROWS_STEP, ROWS_STEP)
            pltpu.make_async_remote_copy(
                src_ref=psnd.at[j, piece],
                dst_ref=eown.at[(1 - core) * half + j, piece],
                send_sem=fsem_s.at[j, r],
                recv_sem=fsem_r.at[j, r],
                device_id={"ctx": partner},
                device_id_type=MESH,
            ).wait_recv()
        row_scores = finish_tile((1 - core) * half + j, row_scores)

    for i in range(tokens // LANES):
        sums[mine, i : i + 1, :] = row_scores[0:1, i * LANES : (i + 1) * LANES]

    def score_copy(k):
        return pltpu.make_async_remote_copy(
            src_ref=sums.at[mine],
            dst_ref=sums.at[mine],
            send_sem=ysem_s.at[k],
            recv_sem=ysem_r.at[k],
            device_id={"head": lax.rem(mine + k, heads_axis)},
            device_id_type=MESH,
        )

    for k in range(1, heads_axis):
        score_copy(k).start()
    for k in range(1, heads_axis):
        score_copy(k).wait()
    total = sums[0]
    for k in range(1, heads_axis):
        total = total + sums[k]
    for i in range(tokens // LANES):
        score_ref[:, i * LANES : (i + 1) * LANES] = total[i : i + 1, :]

    for j in range(half):
        state_copy(sbf, srecv, psem_s, psem_r, j, partner).wait_send()
        for r in range(steps):
            pass_copy(j, r).wait_send()

            @pl.when(chip < last_chip)
            def _():
                chain_copy(j, r).wait_send()
    t_copy.wait_send()


def state_copy(src, dst, send, recv, j, partner):
    return pltpu.make_async_remote_copy(
        src_ref=src.at[j],
        dst_ref=dst.at[j],
        send_sem=send.at[j],
        recv_sem=recv.at[j],
        device_id={"ctx": partner},
        device_id_type=MESH,
    )


def body(inputs, b_proj, c_proj, log_decay, starts, counts, skip_gain, readout):
    tokens, width = inputs.shape[1:]
    ctxs, heads_axis = lax.axis_size("ctx"), lax.axis_size("head")
    tiles = width // LANES
    half = tiles // 2
    spans = tokens // SPAN
    steps = SPAN // ROWS_STEP
    vmem, smem = pl.BlockSpec(memory_space=pltpu.VMEM), pl.BlockSpec(memory_space=pltpu.SMEM)
    big = lambda n, dtype: pltpu.VMEM((n, SPAN, LANES), dtype)
    small = lambda n: pltpu.VMEM((n, 8, LANES), F32)
    sem = pltpu.SemaphoreType.DMA
    return pl.pallas_call(
        functools.partial(kernel, (ctxs, heads_axis, tokens, tiles)),
        out_shape=(
            jax.ShapeDtypeStruct(inputs.shape, BF16),
            jax.ShapeDtypeStruct((1, tokens), F32),
        ),
        in_specs=[smem, vmem, vmem, vmem, vmem, vmem, smem, vmem],
        out_specs=(vmem, vmem),
        scratch_shapes=[
            pltpu.VMEM((tiles, tokens, LANES), BF16),
            pltpu.VMEM((tokens, width), BF16),
            pltpu.VMEM((tiles, tokens, LANES), F32),
            pltpu.VMEM((tokens, LANES), F32),
            pltpu.VMEM((SPAN, tokens), BF16),
            big(tiles, F32),
            big(tiles, F32),
            small(tiles),
            small(tiles),
            big(half, BF16),
            big(half, BF16),
            small(half),
            big(half, F32),
            small(half),
            big(half, F32),
            small(half),
            big(half, BF16),
            big(half, BF16),
            big(tiles, BF16),
            big(half, BF16),
            pltpu.VMEM((tiles, tokens, LANES), F32),
            pltpu.VMEM((spans, SPAN, SPAN), BF16),
            pltpu.VMEM((tokens // SUB, SUB, LANES), F32),
            pltpu.VMEM((heads_axis, tokens // LANES, LANES), F32),
            sem((half,)), sem((half,)), sem((2,)),
            sem((half, steps)), sem((half, steps)),
            sem((half, steps)), sem((half, steps)),
            sem((heads_axis,)), sem((heads_axis,)),
        ],
        compiler_params=pltpu.CompilerParams(collective_id=0, has_side_effects=True),
        name="ssd",
    )(counts, inputs, b_proj, c_proj, log_decay, starts, skip_gain, readout.reshape(1, width))


def solution(mesh):
    placed = (
        P("rep", "ctx", "head"),
        P("rep", "ctx", "head"),
        P("rep", "ctx", "head"),
        P("rep", "head", "ctx"),
        P("rep", "ctx"),
        P("rep", "ctx"),
        P("head"),
        P("head"),
    )
    return jax.shard_map(
        body,
        mesh=mesh,
        in_specs=placed,
        out_specs=(P("rep", "ctx", "head"), P("rep", "ctx")),
        check_vma=False,
    )
```

```python
import functools
import math

import jax
import jax.numpy as jnp
from jax import lax
from jax.experimental import pallas as pl
from jax.experimental.pallas import tpu as pltpu
from jax.sharding import PartitionSpec as P

SPAN = 256
HALF = 128
SUB = 64
LANES = 128
ROWS_STEP = 64
SCORES_AT = 6
EDGES = ((0, 1), (1, 2), (2, 3), (1, 3), (1, 7), (3, 4), (4, 5), (5, 6), (6, 7))
LOG2E = math.log2(math.e)
F32 = jnp.float32
BF16 = jnp.bfloat16
MESH = pl.DeviceIdType.MESH


def mm(a, b):
    return lax.dot_general(a, b, (((1,), (0,)), ((), ())), preferred_element_type=F32)


def mm_nt(a, b):
    return lax.dot_general(a, b, (((1,), (1,)), ((), ())), preferred_element_type=F32)


def mm_tn(a, b):
    return lax.dot_general(a, b, (((0,), (0,)), ((), ())), preferred_element_type=F32)


def iota(shape, dim):
    return lax.broadcasted_iota(jnp.int32, shape, dim)


def kernel(
    sizes,
    count_ref, x_ref, b_ref, c_ref, a_ref, s_ref, gain_ref, read_ref,
    out_ref, score_ref,
    xm, lx, cum, doc, bt, first, whole, ta, td, sbf, srecv, mfull, msnd, mrecv,
    comb, base, mown, mbase, inb, tin, outb, tout, eown, psnd, vent, vsnd, y, gb, gm, sums, rd,
    psem_s, psem_r, tsem, csem_s, csem_r, vsem_s, vsem_r, fsem_s, fsem_r, wsem, ysem_s, ysem_r,
):
    ctxs, heads_axis, tokens, tiles = sizes
    half = tiles // 2
    spans = tokens // SPAN
    steps = SPAN // ROWS_STEP
    ctx = lax.axis_index("ctx")
    core = lax.rem(ctx, 2)
    chip = ctx // 2
    mine = lax.axis_index("head")
    partner = ctx + 1 - 2 * core

    barrier = pltpu.get_barrier_semaphore()
    pl.semaphore_signal(barrier, inc=1, device_id={"ctx": partner}, device_id_type=MESH)
    peers = heads_axis
    for ends in EDGES:
        for here, there in (ends, ends[::-1]):
            peers = peers + jnp.where(chip == here, 1, 0)

            @pl.when(chip == here)
            def _():
                pl.semaphore_signal(
                    barrier, inc=1, device_id={"ctx": 2 * there + core}, device_id_type=MESH
                )

    for k in range(1, heads_axis):
        pl.semaphore_signal(
            barrier, inc=1, device_id={"head": lax.rem(mine + k, heads_axis)}, device_id_type=MESH
        )

    count = count_ref[0, 0]
    live_row = iota((1, tokens), 1) < count
    log_decay = jnp.where(live_row, a_ref[0].astype(F32), 0.0).astype(BF16)
    starts = jnp.where(live_row, s_ref[...].astype(F32), 0.0)
    head_rows = log_decay.shape[0]
    all_starts = jnp.broadcast_to(starts, (head_rows, tokens)).astype(BF16)
    starts = jnp.where(iota((head_rows, tokens), 0) == 0, starts, 0.0).astype(BF16)
    spread = (iota((head_rows, tiles * LANES), 0) == iota((head_rows, tiles * LANES), 1) // SUB)
    spread = jnp.where(spread, 1.0, 0.0).astype(BF16)
    ones = jnp.ones((head_rows, LANES), BF16)
    tri = jnp.where(iota((SPAN, SPAN), 0) >= iota((SPAN, SPAN), 1), 1.0, 0.0).astype(BF16)
    for s in range(spans):
        rows = pl.ds(s * SPAN, SPAN)
        lx[rows, :] = mm_tn(log_decay[:, s * SPAN : (s + 1) * SPAN], spread).astype(BF16)
        spread_starts = mm_tn(starts[:, s * SPAN : (s + 1) * SPAN], ones).astype(BF16)
        doc[rows, :] = mm(tri, spread_starts)
        bt[:, rows] = b_ref[0, rows, :].astype(F32).T.astype(BF16)

    live = iota((tokens, LANES), 0) < count

    rd[...] = read_ref[...].astype(F32)
    upper = jnp.where(iota((SPAN, SPAN), 0) <= iota((SPAN, SPAN), 1), 1.0, 0.0).astype(BF16)
    head_of = iota((head_rows, LANES), 1) // SUB
    read_rows = jnp.zeros((head_rows, tokens), F32)
    for t in range(tiles):
        part = jnp.where(iota((head_rows, LANES), 0) == 2 * t + head_of, rd[t : t + 1, :], 0.0)
        read_rows = read_rows + mm_nt(part.astype(BF16), x_ref[0, :, t * LANES : (t + 1) * LANES])
    read_rows = jnp.where(live_row, read_rows, 0.0)
    enter_rows, read_states, row_totals = [], [], []
    for s in range(spans):
        lanes = slice(s * SPAN, (s + 1) * SPAN)
        run = mm(log_decay[:, lanes], upper) * LOG2E
        docs = mm(all_starts[:, lanes], upper)
        enter_rows.append(jnp.where(docs == 0.0, jnp.exp2(run), 0.0))
        ends = slice(SPAN - 1, SPAN)
        keep = jnp.where(docs == docs[:, ends], jnp.exp2(run[:, ends] - run), 0.0)
        read_states.append(mm((read_rows[:, lanes] * keep).astype(BF16), b_ref[0, pl.ds(s * SPAN, SPAN), :]))
        row_totals.append(jnp.broadcast_to(enter_rows[s][:, ends], (head_rows, LANES)))
    read_state = enter_rows[1][:, SPAN - 1 : SPAN] * read_states[0] + read_states[1]
    for h in range(2):
        rows = slice(h * 8, (h + 1) * 8)
        for i in range(2):
            mfull[h, 1 + i] = read_state[rows, i * LANES : (i + 1) * LANES]
        mfull[h, 3] = row_totals[0][rows] * row_totals[1][rows]

    def state_tile(t):
        cols = pl.ds(pl.multiple_of(t * LANES, LANES), LANES)
        xt = jnp.where(live, x_ref[0, :, cols].astype(F32), 0.0).astype(BF16)
        xm[t] = xt
        states, totals = [], []
        for s in range(spans):
            rows = slice(s * SPAN, (s + 1) * SPAN)
            run = mm(tri, lx[pl.ds(s * SPAN, SPAN), cols]) * LOG2E
            cum[t, pl.ds(s * SPAN, SPAN), :] = run
            docs = doc[pl.ds(s * SPAN, SPAN), :]
            last = run[SPAN - 1 : SPAN, :]
            keep = jnp.where(docs == docs[SPAN - 1 : SPAN, :], jnp.exp2(last - run), 0.0)
            weighted = (xt[rows, :].astype(F32) * keep).astype(BF16)
            states.append(mm(bt[:, pl.ds(s * SPAN, SPAN)], weighted))
            totals.append(jnp.where(docs[SPAN - 1 : SPAN, :] == 0.0, jnp.exp2(last), 0.0))
        first[t] = states[0]
        joined = totals[1] * states[0] + states[1]
        whole[t] = joined
        ta[t] = jnp.broadcast_to(totals[0], (8, LANES))
        td[t] = jnp.broadcast_to(totals[0] * totals[1], (8, LANES))
        return joined

    for j in range(half):
        sbf[j] = state_tile((1 - core) * half + j).astype(BF16)
        if j == 0:
            pl.semaphore_wait(barrier, peers)
        state_copy(sbf, srecv, psem_s, psem_r, j, partner).start()
    t_copy = pltpu.make_async_remote_copy(
        src_ref=msnd,
        dst_ref=mrecv,
        send_sem=tsem.at[0],
        recv_sem=tsem.at[1],
        device_id={"ctx": partner},
        device_id_type=MESH,
    )
    msnd[...] = mfull[1 - core]
    for j in range(half):
        msnd[0, j : j + 1, :] = td[(1 - core) * half + j][0:1, :]
    t_copy.start()
    for j in range(half):
        state_tile(core * half + j)
        mfull[core, 0, j : j + 1, :] = td[core * half + j][0:1, :]

    def join(earlier, later):
        columns = later[3]
        return (
            later[0] * earlier[0],
            columns * earlier[1] + later[1],
            columns * earlier[2] + later[2],
            columns * earlier[3],
        )

    def put(ref, parts):
        for i, part in enumerate(parts):
            ref[i] = part

    def pick(choose, a, b):
        return tuple(jnp.where(choose, u, v) for u, v in zip(a, b))

    def parts_of(ref):
        return tuple(ref[i] for i in range(4))

    t_copy.wait_recv()
    is_low = core == 0
    own_parts, their_parts = parts_of(mfull.at[core]), parts_of(mrecv)
    low_parts, high_parts = pick(is_low, own_parts, their_parts), pick(is_low, their_parts, own_parts)
    put(mown, join(low_parts, high_parts))
    put(mbase, low_parts)
    for j in range(half):
        state_copy(sbf, srecv, psem_s, psem_r, j, partner).wait_recv()
        own, theirs = whole[core * half + j], srecv[j].astype(F32)
        low, high = jnp.where(is_low, own, theirs), jnp.where(is_low, theirs, own)
        comb[j] = high_parts[0][j : j + 1, :] * low + high
        base[j] = low

    def send(src, out, j, r, to, slot):
        piece = rows_of(r)
        return pltpu.make_async_remote_copy(
            src_ref=src.at[j, piece],
            dst_ref=inb.at[slot, j, piece],
            send_sem=csem_s.at[out, j, r],
            recv_sem=csem_r.at[slot, j, r],
            device_id={"ctx": 2 * to + core},
            device_id_type=MESH,
        )

    def send_t(out, to, slot, sem=None):
        return pltpu.make_async_remote_copy(
            src_ref=tout.at[out],
            dst_ref=tin.at[slot],
            send_sem=vsem_s.at[out if sem is None else sem],
            recv_sem=vsem_r.at[slot],
            device_id={"ctx": 2 * to + core},
            device_id_type=MESH,
        )

    def pieces(step, begin=0, end=half * steps):
        def one(q, _):
            step(q // steps, lax.rem(q, steps))
            return 0

        lax.fori_loop(begin, end, one, 0)

    def rows_of(r):
        return pl.ds(pl.multiple_of(r * ROWS_STEP, ROWS_STEP), ROWS_STEP)

    def of_chip(*values):
        result = values[-1]
        for i, value in enumerate(values[:-1]):
            result = jnp.where(chip == i, value, result)
        return result

    def among(*chips):
        return functools.reduce(jnp.logical_or, [chip == i for i in chips])

    to_lead = of_chip(1, 0, 3, 2, 5, 4, 4, 4)
    to_join = of_chip(1, 3, 1, 1, 4, 6, 7, 6)
    join_slot = jnp.where(chip < 3, 1, 0)
    to_last = of_chip(1, 7, 1, 4, 5, 4, 4, 6)

    def pass_copy(j, r):
        piece = rows_of(r)
        return pltpu.make_async_remote_copy(
            src_ref=psnd.at[j, piece],
            dst_ref=eown.at[core * half + j, piece],
            send_sem=fsem_s.at[j, r],
            recv_sem=fsem_r.at[j, r],
            device_id={"ctx": partner},
            device_id_type=MESH,
        )

    def local_part():
        for s in range(spans):
            rows = pl.ds(s * SPAN, SPAN)
            scores = mm_nt(c_ref[0, rows, :], b_ref[0, rows, :])
            gb[s] = scores.astype(BF16)
        lane = iota((SUB, LANES), 1)
        lane = jnp.where(lane < SUB, lane, lane - SUB)
        row = iota((SUB, LANES), 0)
        eye = jnp.where(row == lane, 1.0, 0.0)
        for k in range(tokens // SUB):
            rows = pl.ds(k * SUB, SUB)
            bk = b_ref[0, rows, :]
            sc = mm_nt(c_ref[0, rows, :], jnp.concatenate([bk, bk], axis=0))
            dk = doc[rows, :]
            drow = jnp.sum(dk * eye, axis=0, keepdims=True)
            gm[k] = jnp.where((row >= lane) & (dk == drow), sc, 0.0)
        low_lane = iota((SUB, LANES), 1) < SUB
        one_lane = iota((1, LANES), 1) < SUB

        def tile(t, _):
            skip = jnp.where(one_lane, gain_ref[2 * t], gain_ref[2 * t + 1])
            for s in range(spans):
                o = s * SPAN

                def level(at, width):
                    lo, hi = pl.ds(o + at, width), pl.ds(o + at + width, width)
                    run_lo, run_hi = cum[t, lo, :], cum[t, hi, :]
                    doc_lo, doc_hi = doc[lo, :], doc[hi, :]
                    ref, ref_doc = run_lo[width - 1 : width, :], doc_lo[width - 1 : width, :]
                    keep = jnp.where(doc_lo == ref_doc, jnp.exp2(ref - run_lo), 0.0)
                    enter = jnp.where(doc_hi == ref_doc, jnp.exp2(run_hi - ref), 0.0)
                    weighted = (xm[t, lo, :].astype(F32) * keep).astype(BF16)
                    part = gb[s, at + width : at + 2 * width, at : at + width]
                    return enter * mm(part, weighted)

                far = level(0, HALF)
                near = [level(0, SUB), level(HALF, SUB)]
                for q in range(SPAN // SUB):
                    rows = pl.ds(o + q * SUB, SUB)
                    run = cum[t, rows, :]
                    xq = xm[t, rows, :]
                    xf = xq.astype(F32)
                    run_row = jnp.sum(run * eye, axis=0, keepdims=True)
                    w = jnp.exp2(jnp.minimum(run - run_row, 0.0)) * gm[s * (SPAN // SUB) + q]
                    left = jnp.where(low_lane, xf, 0.0).astype(BF16)
                    right = jnp.where(low_lane, 0.0, xf).astype(BF16)
                    v = mm(w.astype(BF16), jnp.concatenate([left, right], axis=0))
                    v = v + skip * xf
                    if q % 2 == 1:
                        v = v + near[q // 2]
                    if q >= 2:
                        v = v + far[(q - 2) * SUB : (q - 1) * SUB, :]
                    y[t, rows, :] = v
            return 0

        lax.fori_loop(0, tiles, tile, 0)

    @pl.when(among(0, 2, 3, 4))
    def _():
        tout[0] = mown[...]
        send_t(0, to_lead, 0).start()

        def step(j, r):
            piece = rows_of(r)
            outb[0, j, piece, :] = comb[j, piece, :].astype(BF16)
            send(outb.at[0], 0, j, r, to_lead, 0).start()

        pieces(step)

    local_part()

    @pl.when(among(1, 2, 3, 5, 6, 7))
    def _():
        send_t(0, to_lead, 0).wait_recv()

    def row(ref, j):
        return ref[0, pl.ds(j, 1), :]

    is_later = chip == 2

    @pl.when(among(1, 2, 5, 6))
    def _():
        got, own = parts_of(tin.at[0]), parts_of(mown)
        put(tout.at[1], join(pick(is_later, own, got), pick(is_later, got, own)))
        send_t(1, to_join, join_slot).start()

    def join_step(j, r):
        piece = rows_of(r)
        send(outb.at[0], 0, j, r, to_lead, 0).wait_recv()
        got, own = inb[0, j, piece, :].astype(F32), comb[j, piece, :]
        scale = jnp.where(is_later, row(tin.at[0], j), row(mown, j))
        joined = scale * jnp.where(is_later, own, got) + jnp.where(is_later, got, own)
        outb[1, j, piece, :] = joined.astype(BF16)
        send(outb.at[1], 1, j, r, to_join, join_slot).start()

    @pl.when(among(2, 5, 6))
    def _():
        pieces(join_step)

    def enter(j, r, e):
        piece = rows_of(r)
        f = row(mbase, j) * e + base[j, piece, :]
        eown[core * half + j, piece, :] = jnp.where(is_low, e, f).astype(BF16)
        psnd[j, piece, :] = jnp.where(is_low, f, e).astype(BF16)
        pass_copy(j, r).start()

    def pass_rows(side):
        return pltpu.make_async_remote_copy(
            src_ref=vsnd,
            dst_ref=vent.at[side],
            send_sem=wsem.at[0],
            recv_sem=wsem.at[1],
            device_id={"ctx": partner},
            device_id_type=MESH,
        )

    def enter_rows_of(e):
        for i in range(2):
            f = mbase[3] * e[i] + mbase[1 + i]
            vent[core, i] = jnp.where(is_low, e[i], f)
            vsnd[i] = jnp.where(is_low, f, e[i])
        pass_rows(core).start()

    @pl.when(chip == 0)
    def _():
        enter_rows_of((jnp.zeros((8, LANES), F32),) * 2)
        pieces(lambda j, r: enter(j, r, jnp.zeros((ROWS_STEP, LANES), F32)))

    @pl.when(chip == 1)
    def _():
        enter_rows_of((tin[0, 1], tin[0, 2]))

        def last_step(j, r):
            piece = rows_of(r)
            send(outb.at[1], 1, j, r, 1, 1).wait_recv()
            got, own = inb[1, j, piece, :].astype(F32), outb[1, j, piece, :].astype(F32)
            outb[2, j, piece, :] = (row(tin.at[1], j) * own + got).astype(BF16)
            send(outb.at[2], 2, j, r, 7, 1).start()

        def both(j, r):
            join_step(j, r)
            last_step(j - behind // steps, r)

        behind = (half // 2) * steps
        pieces(join_step, 0, behind)
        send_t(1, 1, 1).wait_recv()
        put(tout.at[2], join(parts_of(tout.at[1]), parts_of(tin.at[1])))
        send_t(2, 7, 1).start()
        pieces(both, behind, half * steps)
        send_t(1, 2, 1, 3).start()
        pieces(lambda j, r: send(outb.at[1], 3, j, r, 2, 1).start())
        pieces(last_step, half * steps - behind, half * steps)
        pieces(lambda j, r: enter(j, r, inb[0, j, rows_of(r), :].astype(F32)))

    joins = among(3, 5, 6, 7)

    def last_step(j, r):
        piece = rows_of(r)
        send(outb.at[2], 2, j, r, 1, 1).wait_recv()

        @pl.when(among(4, 7))
        def _():
            send(inb.at[1], 2, j, r, to_last, 1).start()

        @pl.when(among(3, 7))
        def _():
            send(outb.at[0], 0, j, r, to_lead, 0).wait_recv()

        got = inb[1, j, piece, :].astype(F32)
        add = jnp.where(joins, inb[0, j, piece, :].astype(F32), 0.0)
        e = jnp.where(joins, row(tin.at[0], j), 1.0) * got + add

        @pl.when(chip == 3)
        def _():
            outb[2, j, piece, :] = (row(mown, j) * e + comb[j, piece, :]).astype(BF16)
            send(outb.at[2], 2, j, r, 4, 1).start()

        enter(j, r, e)

    @pl.when(chip >= 2)
    def _():
        send_t(2, 1, 1).wait_recv()

        @pl.when(among(4, 7))
        def _():
            tout[2] = tin[1]
            send_t(2, to_last, 1).start()

        e = parts_of(tin.at[1])
        e = pick(joins, join(e, parts_of(tin.at[0])), e)

        @pl.when(chip == 3)
        def _():
            put(tout.at[2], join(e, parts_of(mown)))
            send_t(2, to_last, 1).start()

        enter_rows_of(e[1:3])
        pieces(last_step, 0, SCORES_AT)

    pass_rows(1 - core).wait_recv()
    entering = jnp.concatenate(
        [jnp.concatenate([vent[h, 0], vent[h, 1]], axis=1) for h in range(2)], axis=0
    )
    local_rows = jnp.zeros((head_rows, tokens), F32)
    for t in range(tiles):
        weight = jnp.broadcast_to(rd[t : t + 1, :], (head_rows, LANES)).astype(BF16)
        local_rows = local_rows + mm_nt(weight, y[t].astype(BF16))
    row_scores = []
    for s in range(spans):
        if s > 0:
            entering = enter_rows[0][:, SPAN - 1 : SPAN] * entering + read_states[0]
        far = mm_nt(entering.astype(BF16), c_ref[0, pl.ds(s * SPAN, SPAN), :]) * enter_rows[s]
        far = jnp.sum(far, axis=0, keepdims=True)
        row_scores.append(far + local_rows[0:1, s * SPAN : (s + 1) * SPAN])
    row_scores = jnp.where(live_row, jnp.concatenate(row_scores, axis=1), 0.0)
    for i in range(tokens // LANES):
        sums[mine, i : i + 1, :] = row_scores[:, i * LANES : (i + 1) * LANES]

    def score_copy(k):
        return pltpu.make_async_remote_copy(
            src_ref=sums.at[mine],
            dst_ref=sums.at[mine],
            send_sem=ysem_s.at[k],
            recv_sem=ysem_r.at[k],
            device_id={"head": lax.rem(mine + k, heads_axis)},
            device_id_type=MESH,
        )

    for k in range(1, heads_axis):
        score_copy(k).start()

    @pl.when(chip >= 2)
    def _():
        pieces(last_step, SCORES_AT, half * steps)

    def finish_tile(t):
        cols = pl.ds(pl.multiple_of(t * LANES, LANES), LANES)
        e0 = eown[t]
        e1 = (ta[t][0:1, :] * e0.astype(F32) + first[t]).astype(BF16)
        for s, e in enumerate((e0, e1)):
            rows = pl.ds(s * SPAN, SPAN)
            enter = jnp.where(doc[rows, :] == 0.0, jnp.exp2(cum[t, rows, :]), 0.0)
            v = y[t, rows, :] + enter * mm(c_ref[0, rows, :], e)
            v = jnp.where(live[s * SPAN : (s + 1) * SPAN, :], v, 0.0).astype(BF16)
            out_ref[0, rows, cols] = v

    for j in range(half):
        finish_tile(core * half + j)
    for j in range(half):
        for r in range(steps):
            piece = pl.ds(r * ROWS_STEP, ROWS_STEP)
            pltpu.make_async_remote_copy(
                src_ref=psnd.at[j, piece],
                dst_ref=eown.at[(1 - core) * half + j, piece],
                send_sem=fsem_s.at[j, r],
                recv_sem=fsem_r.at[j, r],
                device_id={"ctx": partner},
                device_id_type=MESH,
            ).wait_recv()
        finish_tile((1 - core) * half + j)

    for k in range(1, heads_axis):
        score_copy(k).wait()
    total = sums[0]
    for k in range(1, heads_axis):
        total = total + sums[k]
    for i in range(tokens // LANES):
        score_ref[:, i * LANES : (i + 1) * LANES] = total[i : i + 1, :]

    for j in range(half):
        state_copy(sbf, srecv, psem_s, psem_r, j, partner).wait_send()
    t_copy.wait_send()
    pieces(lambda j, r: pass_copy(j, r).wait_send())

    @pl.when(among(0, 2, 3, 4))
    def _():
        send_t(0, to_lead, 0).wait_send()
        pieces(lambda j, r: send(outb.at[0], 0, j, r, to_lead, 0).wait_send())

    pass_rows(core).wait_send()

    @pl.when(among(1, 2, 5, 6))
    def _():
        send_t(1, to_join, join_slot).wait_send()
        pieces(lambda j, r: send(outb.at[1], 1, j, r, to_join, join_slot).wait_send())

    @pl.when(among(1, 3, 4, 7))
    def _():
        send_t(2, to_last, 1).wait_send()
        pieces(lambda j, r: send(outb.at[2], 2, j, r, to_last, 1).wait_send())

    @pl.when(chip == 1)
    def _():
        send_t(1, 2, 1, 3).wait_send()
        pieces(lambda j, r: send(outb.at[1], 3, j, r, 2, 1).wait_send())


def state_copy(src, dst, send, recv, j, partner):
    return pltpu.make_async_remote_copy(
        src_ref=src.at[j],
        dst_ref=dst.at[j],
        send_sem=send.at[j],
        recv_sem=recv.at[j],
        device_id={"ctx": partner},
        device_id_type=MESH,
    )


def body(inputs, b_proj, c_proj, log_decay, starts, counts, skip_gain, readout):
    tokens, width = inputs.shape[1:]
    ctxs, heads_axis = lax.axis_size("ctx"), lax.axis_size("head")
    tiles = width // LANES
    half = tiles // 2
    spans = tokens // SPAN
    steps = SPAN // ROWS_STEP
    vmem, smem = pl.BlockSpec(memory_space=pltpu.VMEM), pl.BlockSpec(memory_space=pltpu.SMEM)
    big = lambda n, dtype: pltpu.VMEM((n, SPAN, LANES), dtype)
    small = lambda n: pltpu.VMEM((n, 8, LANES), F32)
    sem = pltpu.SemaphoreType.DMA
    return pl.pallas_call(
        functools.partial(kernel, (ctxs, heads_axis, tokens, tiles)),
        out_shape=(
            jax.ShapeDtypeStruct(inputs.shape, BF16),
            jax.ShapeDtypeStruct((1, tokens), F32),
        ),
        in_specs=[smem, vmem, vmem, vmem, vmem, vmem, smem, vmem],
        out_specs=(vmem, vmem),
        scratch_shapes=[
            pltpu.VMEM((tiles, tokens, LANES), BF16),
            pltpu.VMEM((tokens, width), BF16),
            pltpu.VMEM((tiles, tokens, LANES), F32),
            pltpu.VMEM((tokens, LANES), F32),
            pltpu.VMEM((SPAN, tokens), BF16),
            big(tiles, F32),
            big(tiles, F32),
            small(tiles),
            small(tiles),
            big(half, BF16),
            big(half, BF16),
            pltpu.VMEM((2, 4, 8, LANES), F32),
            small(4),
            small(4),
            big(half, F32),
            big(half, F32),
            small(4),
            small(4),
            pltpu.VMEM((2, half, SPAN, LANES), BF16),
            pltpu.VMEM((2, 4, 8, LANES), F32),
            pltpu.VMEM((3, half, SPAN, LANES), BF16),
            pltpu.VMEM((3, 4, 8, LANES), F32),
            big(tiles, BF16),
            big(half, BF16),
            pltpu.VMEM((2, 2, 8, LANES), F32),
            small(2),
            pltpu.VMEM((tiles, tokens, LANES), F32),
            pltpu.VMEM((spans, SPAN, SPAN), BF16),
            pltpu.VMEM((tokens // SUB, SUB, LANES), F32),
            pltpu.VMEM((heads_axis, tokens // LANES, LANES), F32),
            pltpu.VMEM((tiles, LANES), F32),
            sem((half,)), sem((half,)), sem((2,)),
            sem((4, half, steps)), sem((2, half, steps)), sem((4,)), sem((2,)),
            sem((half, steps)), sem((half, steps)), sem((2,)),
            sem((heads_axis,)), sem((heads_axis,)),
        ],
        compiler_params=pltpu.CompilerParams(collective_id=0, has_side_effects=True),
        name="ssd",
    )(counts, inputs, b_proj, c_proj, log_decay, starts, skip_gain, readout.reshape(tiles, LANES))


def solution(mesh):
    placed = (
        P("rep", "ctx", "head"),
        P("rep", "ctx", "head"),
        P("rep", "ctx", "head"),
        P("rep", "head", "ctx"),
        P("rep", "ctx"),
        P("rep", "ctx"),
        P("head"),
        P("head"),
    )
    return jax.shard_map(
        body,
        mesh=mesh,
        in_specs=placed,
        out_specs=(P("rep", "ctx", "head"), P("rep", "ctx")),
        check_vma=False,
    )
```

```python
import functools
import math

import jax
import jax.numpy as jnp
from jax import lax
from jax.experimental import pallas as pl
from jax.experimental.pallas import tpu as pltpu
from jax.sharding import PartitionSpec as P

SPAN = 256
HALF = 128
SUB = 64
LANES = 128
ROWS_STEP = 64
SCORES_AT = 6
DIRECT = 4
EDGES = ((0, 1), (1, 2), (2, 3), (1, 3), (1, 6), (1, 7), (3, 4), (3, 5), (4, 5), (5, 6), (6, 7))
LOG2E = math.log2(math.e)
F32 = jnp.float32
BF16 = jnp.bfloat16
MESH = pl.DeviceIdType.MESH


def mm(a, b):
    return lax.dot_general(a, b, (((1,), (0,)), ((), ())), preferred_element_type=F32)


def mm_nt(a, b):
    return lax.dot_general(a, b, (((1,), (1,)), ((), ())), preferred_element_type=F32)


def mm_tn(a, b):
    return lax.dot_general(a, b, (((0,), (0,)), ((), ())), preferred_element_type=F32)


def iota(shape, dim):
    return lax.broadcasted_iota(jnp.int32, shape, dim)


def kernel(
    sizes,
    count_ref, x_hbm, b_hbm, c_hbm, a_hbm, s_hbm, gain_ref, read_hbm,
    out_ref, score_ref,
    x_ref, b_ref, c_ref, a_ref, s_ref, read_ref, isem,
    xm, lx, cum, doc, bt, first, whole, ta, td, sbf, srecv, mfull, msnd, mrecv,
    comb, base, mown, mbase, inb, tin, outb, tout, eown, psnd, vent, vsnd, y, gb, gm, sums, rd,
    psem_s, psem_r, tsem, csem_s, csem_r, vsem_s, vsem_r, fsem_s, fsem_r, wsem, ysem_s, ysem_r,
):
    ctxs, heads_axis, tokens, tiles = sizes
    half = tiles // 2
    spans = tokens // SPAN
    steps = SPAN // ROWS_STEP
    ctx = lax.axis_index("ctx")
    core = lax.rem(ctx, 2)
    chip = ctx // 2
    mine = lax.axis_index("head")
    partner = ctx + 1 - 2 * core

    loads = [
        pltpu.make_async_copy(source, target, isem.at[i])
        for i, (source, target) in enumerate(
            ((a_hbm, a_ref), (s_hbm, s_ref), (read_hbm, read_ref), (b_hbm, b_ref), (x_hbm, x_ref), (c_hbm, c_ref))
        )
    ]
    for load in loads:
        load.start()
    barrier = pltpu.get_barrier_semaphore()
    pl.semaphore_signal(barrier, inc=1, device_id={"ctx": partner}, device_id_type=MESH)
    peers = heads_axis
    for ends in EDGES:
        for here, there in (ends, ends[::-1]):
            peers = peers + jnp.where(chip == here, 1, 0)

            @pl.when(chip == here)
            def _():
                pl.semaphore_signal(
                    barrier, inc=1, device_id={"ctx": 2 * there + core}, device_id_type=MESH
                )

    for k in range(1, heads_axis):
        pl.semaphore_signal(
            barrier, inc=1, device_id={"head": lax.rem(mine + k, heads_axis)}, device_id_type=MESH
        )

    count = count_ref[0, 0]
    live_row = iota((1, tokens), 1) < count
    loads[0].wait()
    loads[1].wait()
    log_decay = jnp.where(live_row, a_ref[0].astype(F32), 0.0).astype(BF16)
    starts = jnp.where(live_row, s_ref[...].astype(F32), 0.0)
    head_rows = log_decay.shape[0]
    all_starts = jnp.broadcast_to(starts, (head_rows, tokens)).astype(BF16)
    starts = jnp.where(iota((head_rows, tokens), 0) == 0, starts, 0.0).astype(BF16)
    spread = (iota((head_rows, tiles * LANES), 0) == iota((head_rows, tiles * LANES), 1) // SUB)
    spread = jnp.where(spread, 1.0, 0.0).astype(BF16)
    ones = jnp.ones((head_rows, LANES), BF16)
    tri = jnp.where(iota((SPAN, SPAN), 0) >= iota((SPAN, SPAN), 1), 1.0, 0.0).astype(BF16)
    for s in range(spans):
        rows = pl.ds(s * SPAN, SPAN)
        lx[rows, :] = mm_tn(log_decay[:, s * SPAN : (s + 1) * SPAN], spread).astype(BF16)
        spread_starts = mm_tn(starts[:, s * SPAN : (s + 1) * SPAN], ones).astype(BF16)
        doc[rows, :] = mm(tri, spread_starts)
    loads[3].wait()
    for s in range(spans):
        rows = pl.ds(s * SPAN, SPAN)
        bt[:, rows] = b_ref[0, rows, :].astype(F32).T.astype(BF16)
    loads[2].wait()
    loads[4].wait()

    live = iota((tokens, LANES), 0) < count

    rd[...] = read_ref[...].astype(F32)
    upper = jnp.where(iota((SPAN, SPAN), 0) <= iota((SPAN, SPAN), 1), 1.0, 0.0).astype(BF16)
    head_of = iota((head_rows, LANES), 1) // SUB
    read_rows = jnp.zeros((head_rows, tokens), F32)
    for t in range(tiles):
        part = jnp.where(iota((head_rows, LANES), 0) == 2 * t + head_of, rd[t : t + 1, :], 0.0)
        read_rows = read_rows + mm_nt(part.astype(BF16), x_ref[0, :, t * LANES : (t + 1) * LANES])
    read_rows = jnp.where(live_row, read_rows, 0.0)
    enter_rows, read_states, row_totals = [], [], []
    for s in range(spans):
        lanes = slice(s * SPAN, (s + 1) * SPAN)
        run = mm(log_decay[:, lanes], upper) * LOG2E
        docs = mm(all_starts[:, lanes], upper)
        enter_rows.append(jnp.where(docs == 0.0, jnp.exp2(run), 0.0))
        ends = slice(SPAN - 1, SPAN)
        keep = jnp.where(docs == docs[:, ends], jnp.exp2(run[:, ends] - run), 0.0)
        read_states.append(mm((read_rows[:, lanes] * keep).astype(BF16), b_ref[0, pl.ds(s * SPAN, SPAN), :]))
        row_totals.append(jnp.broadcast_to(enter_rows[s][:, ends], (head_rows, LANES)))
    read_state = enter_rows[1][:, SPAN - 1 : SPAN] * read_states[0] + read_states[1]
    for h in range(2):
        rows = slice(h * 8, (h + 1) * 8)
        for i in range(2):
            mfull[h, 1 + i] = read_state[rows, i * LANES : (i + 1) * LANES]
        mfull[h, 3] = row_totals[0][rows] * row_totals[1][rows]

    def state_tile(t):
        cols = pl.ds(pl.multiple_of(t * LANES, LANES), LANES)
        xt = jnp.where(live, x_ref[0, :, cols].astype(F32), 0.0).astype(BF16)
        xm[t] = xt
        states, totals = [], []
        for s in range(spans):
            rows = slice(s * SPAN, (s + 1) * SPAN)
            run = mm(tri, lx[pl.ds(s * SPAN, SPAN), cols]) * LOG2E
            cum[t, pl.ds(s * SPAN, SPAN), :] = run
            docs = doc[pl.ds(s * SPAN, SPAN), :]
            last = run[SPAN - 1 : SPAN, :]
            keep = jnp.where(docs == docs[SPAN - 1 : SPAN, :], jnp.exp2(last - run), 0.0)
            weighted = (xt[rows, :].astype(F32) * keep).astype(BF16)
            states.append(mm(bt[:, pl.ds(s * SPAN, SPAN)], weighted))
            totals.append(jnp.where(docs[SPAN - 1 : SPAN, :] == 0.0, jnp.exp2(last), 0.0))
        first[t] = states[0]
        joined = totals[1] * states[0] + states[1]
        whole[t] = joined
        ta[t] = jnp.broadcast_to(totals[0], (8, LANES))
        td[t] = jnp.broadcast_to(totals[0] * totals[1], (8, LANES))
        return joined

    for j in range(half):
        sbf[j] = state_tile((1 - core) * half + j).astype(BF16)
        if j == 0:
            pl.semaphore_wait(barrier, peers)
        state_copy(sbf, srecv, psem_s, psem_r, j, partner).start()
    t_copy = pltpu.make_async_remote_copy(
        src_ref=msnd,
        dst_ref=mrecv,
        send_sem=tsem.at[0],
        recv_sem=tsem.at[1],
        device_id={"ctx": partner},
        device_id_type=MESH,
    )
    msnd[...] = mfull[1 - core]
    for j in range(half):
        msnd[0, j : j + 1, :] = td[(1 - core) * half + j][0:1, :]
    t_copy.start()
    for j in range(half):
        state_tile(core * half + j)
        mfull[core, 0, j : j + 1, :] = td[core * half + j][0:1, :]

    def join(earlier, later):
        columns = later[3]
        return (
            later[0] * earlier[0],
            columns * earlier[1] + later[1],
            columns * earlier[2] + later[2],
            columns * earlier[3],
        )

    def put(ref, parts):
        for i, part in enumerate(parts):
            ref[i] = part

    def pick(choose, a, b):
        return tuple(jnp.where(choose, u, v) for u, v in zip(a, b))

    def parts_of(ref):
        return tuple(ref[i] for i in range(4))

    t_copy.wait_recv()
    is_low = core == 0
    own_parts, their_parts = parts_of(mfull.at[core]), parts_of(mrecv)
    low_parts, high_parts = pick(is_low, own_parts, their_parts), pick(is_low, their_parts, own_parts)
    put(mown, join(low_parts, high_parts))
    put(mbase, low_parts)
    for j in range(half):
        state_copy(sbf, srecv, psem_s, psem_r, j, partner).wait_recv()
        own, theirs = whole[core * half + j], srecv[j].astype(F32)
        low, high = jnp.where(is_low, own, theirs), jnp.where(is_low, theirs, own)
        comb[j] = high_parts[0][j : j + 1, :] * low + high
        base[j] = low

    def send(src, out, j, r, to, slot):
        piece = rows_of(r)
        return pltpu.make_async_remote_copy(
            src_ref=src.at[j, piece],
            dst_ref=inb.at[slot, j, piece],
            send_sem=csem_s.at[out, j, r],
            recv_sem=csem_r.at[slot, j, r],
            device_id={"ctx": 2 * to + core},
            device_id_type=MESH,
        )

    def send_t(out, to, slot):
        return pltpu.make_async_remote_copy(
            src_ref=tout.at[out],
            dst_ref=tin.at[slot],
            send_sem=vsem_s.at[out],
            recv_sem=vsem_r.at[slot],
            device_id={"ctx": 2 * to + core},
            device_id_type=MESH,
        )

    def back_t():
        return pltpu.make_async_remote_copy(
            src_ref=tin.at[1],
            dst_ref=tin.at[1],
            send_sem=vsem_s.at[3],
            recv_sem=vsem_r.at[1],
            device_id={"ctx": 4 + core},
            device_id_type=MESH,
        )

    def pieces(step, begin=0, end=half * steps):
        def one(q, _):
            step(q // steps, lax.rem(q, steps))
            return 0

        lax.fori_loop(begin, end, one, 0)

    def rows_of(r):
        return pl.ds(pl.multiple_of(r * ROWS_STEP, ROWS_STEP), ROWS_STEP)

    def of_chip(*values):
        result = values[-1]
        for i, value in enumerate(values[:-1]):
            result = jnp.where(chip == i, value, result)
        return result

    def among(*chips):
        return functools.reduce(jnp.logical_or, [chip == i for i in chips])

    to_lead = of_chip(1, 0, 3, 2, 5, 4, 4, 4)
    to_join = of_chip(1, 3, 1, 1, 4, 6, 7, 6)
    join_slot = jnp.where(chip < 3, 1, 0)
    to_last = of_chip(1, 7, 1, 4, 5, 4, 4, 6)

    def pass_copy(j, r):
        piece = rows_of(r)
        return pltpu.make_async_remote_copy(
            src_ref=psnd.at[j, piece],
            dst_ref=eown.at[core * half + j, piece],
            send_sem=fsem_s.at[j, r],
            recv_sem=fsem_r.at[j, r],
            device_id={"ctx": partner},
            device_id_type=MESH,
        )

    def local_part():
        loads[5].wait()
        for s in range(spans):
            rows = pl.ds(s * SPAN, SPAN)
            scores = mm_nt(c_ref[0, rows, :], b_ref[0, rows, :])
            gb[s] = scores.astype(BF16)
        lane = iota((SUB, LANES), 1)
        lane = jnp.where(lane < SUB, lane, lane - SUB)
        row = iota((SUB, LANES), 0)
        eye = jnp.where(row == lane, 1.0, 0.0)
        for k in range(tokens // SUB):
            rows = pl.ds(k * SUB, SUB)
            bk = b_ref[0, rows, :]
            sc = mm_nt(c_ref[0, rows, :], jnp.concatenate([bk, bk], axis=0))
            dk = doc[rows, :]
            drow = jnp.sum(dk * eye, axis=0, keepdims=True)
            gm[k] = jnp.where((row >= lane) & (dk == drow), sc, 0.0)
        low_lane = iota((SUB, LANES), 1) < SUB
        one_lane = iota((1, LANES), 1) < SUB

        def tile(t, _):
            skip = jnp.where(one_lane, gain_ref[2 * t], gain_ref[2 * t + 1])
            for s in range(spans):
                o = s * SPAN

                def level(at, width):
                    lo, hi = pl.ds(o + at, width), pl.ds(o + at + width, width)
                    run_lo, run_hi = cum[t, lo, :], cum[t, hi, :]
                    doc_lo, doc_hi = doc[lo, :], doc[hi, :]
                    ref, ref_doc = run_lo[width - 1 : width, :], doc_lo[width - 1 : width, :]
                    keep = jnp.where(doc_lo == ref_doc, jnp.exp2(ref - run_lo), 0.0)
                    enter = jnp.where(doc_hi == ref_doc, jnp.exp2(run_hi - ref), 0.0)
                    weighted = (xm[t, lo, :].astype(F32) * keep).astype(BF16)
                    part = gb[s, at + width : at + 2 * width, at : at + width]
                    return enter * mm(part, weighted)

                far = level(0, HALF)
                near = [level(0, SUB), level(HALF, SUB)]
                for q in range(SPAN // SUB):
                    rows = pl.ds(o + q * SUB, SUB)
                    run = cum[t, rows, :]
                    xq = xm[t, rows, :]
                    xf = xq.astype(F32)
                    run_row = jnp.sum(run * eye, axis=0, keepdims=True)
                    w = jnp.exp2(jnp.minimum(run - run_row, 0.0)) * gm[s * (SPAN // SUB) + q]
                    left = jnp.where(low_lane, xf, 0.0).astype(BF16)
                    right = jnp.where(low_lane, 0.0, xf).astype(BF16)
                    v = mm(w.astype(BF16), jnp.concatenate([left, right], axis=0))
                    v = v + skip * xf
                    if q % 2 == 1:
                        v = v + near[q // 2]
                    if q >= 2:
                        v = v + far[(q - 2) * SUB : (q - 1) * SUB, :]
                    y[t, rows, :] = v
            return 0

        lax.fori_loop(0, tiles, tile, 0)

    @pl.when(among(0, 2, 3, 4))
    def _():
        tout[0] = mown[...]
        send_t(0, to_lead, 0).start()

        def step(j, r):
            piece = rows_of(r)
            outb[0, j, piece, :] = comb[j, piece, :].astype(BF16)
            send(outb.at[0], 0, j, r, to_lead, 0).start()

        pieces(step)

    local_part()

    @pl.when(among(1, 2, 3, 5, 6, 7))
    def _():
        send_t(0, to_lead, 0).wait_recv()

    def row(ref, j):
        return ref[0, pl.ds(j, 1), :]

    is_later = chip == 2

    @pl.when(among(1, 2, 5, 6))
    def _():
        got, own = parts_of(tin.at[0]), parts_of(mown)
        put(tout.at[1], join(pick(is_later, own, got), pick(is_later, got, own)))
        send_t(1, to_join, join_slot).start()

    def join_step(j, r):
        piece = rows_of(r)
        send(outb.at[0], 0, j, r, to_lead, 0).wait_recv()
        got, own = inb[0, j, piece, :].astype(F32), comb[j, piece, :]
        scale = jnp.where(is_later, row(tin.at[0], j), row(mown, j))
        joined = scale * jnp.where(is_later, own, got) + jnp.where(is_later, got, own)
        outb[1, j, piece, :] = joined.astype(BF16)
        send(outb.at[1], 1, j, r, to_join, join_slot).start()

    @pl.when(among(2, 5, 6))
    def _():
        pieces(join_step)

    def enter(j, r, e):
        piece = rows_of(r)
        f = row(mbase, j) * e + base[j, piece, :]
        eown[core * half + j, piece, :] = jnp.where(is_low, e, f).astype(BF16)
        psnd[j, piece, :] = jnp.where(is_low, f, e).astype(BF16)
        pass_copy(j, r).start()

    def pass_rows(side):
        return pltpu.make_async_remote_copy(
            src_ref=vsnd,
            dst_ref=vent.at[side],
            send_sem=wsem.at[0],
            recv_sem=wsem.at[1],
            device_id={"ctx": partner},
            device_id_type=MESH,
        )

    def enter_rows_of(e):
        for i in range(2):
            f = mbase[3] * e[i] + mbase[1 + i]
            vent[core, i] = jnp.where(is_low, e[i], f)
            vsnd[i] = jnp.where(is_low, f, e[i])
        pass_rows(core).start()

    @pl.when(chip == 0)
    def _():
        enter_rows_of((jnp.zeros((8, LANES), F32),) * 2)
        pieces(lambda j, r: enter(j, r, jnp.zeros((ROWS_STEP, LANES), F32)))

    def direct(j, r, to):
        @pl.when(j * steps + r >= half * steps - DIRECT)
        def _():
            send(outb.at[2], 3, j, r, to, 1).start()

    rest = []

    @pl.when(chip == 1)
    def _():
        enter_rows_of((tin[0, 1], tin[0, 2]))

        def last_step(j, r):
            piece = rows_of(r)
            send(outb.at[1], 1, j, r, 1, 1).wait_recv()
            got, own = inb[1, j, piece, :].astype(F32), outb[1, j, piece, :].astype(F32)
            outb[2, j, piece, :] = (row(tin.at[1], j) * own + got).astype(BF16)
            send(outb.at[2], 2, j, r, 7, 1).start()
            direct(j, r, 6)

        def both(j, r):
            join_step(j, r)
            last_step(j - behind // steps, r)

        behind = (half // 2) * steps
        pieces(join_step, 0, behind)
        send_t(1, 1, 1).wait_recv()
        put(tout.at[2], join(parts_of(tout.at[1]), parts_of(tin.at[1])))
        send_t(2, 7, 1).start()
        pieces(both, behind, half * steps)
        rest.append(lambda: pieces(last_step, half * steps - behind, half * steps))
        rest.append(lambda: pieces(lambda j, r: enter(j, r, inb[0, j, rows_of(r), :].astype(F32))))

    joins = among(3, 5, 6, 7)

    def last_step(j, r):
        piece = rows_of(r)
        send(outb.at[2], 2, j, r, 1, 1).wait_recv()

        @pl.when(among(4, 7) & (j * steps + r < half * steps - DIRECT))
        def _():
            send(inb.at[1], 2, j, r, to_last, 1).start()

        @pl.when(among(3, 7))
        def _():
            send(outb.at[0], 0, j, r, to_lead, 0).wait_recv()

        got = inb[1, j, piece, :].astype(F32)
        add = jnp.where(joins, inb[0, j, piece, :].astype(F32), 0.0)
        e = jnp.where(joins, row(tin.at[0], j), 1.0) * got + add

        @pl.when(chip == 3)
        def _():
            outb[2, j, piece, :] = (row(mown, j) * e + comb[j, piece, :]).astype(BF16)
            send(outb.at[2], 2, j, r, 4, 1).start()
            direct(j, r, 5)
            send(inb.at[1], 4, j, r, 2, 1).start()

        enter(j, r, e)

    @pl.when(chip >= 2)
    def _():
        send_t(2, 1, 1).wait_recv()

        @pl.when(among(4, 7))
        def _():
            tout[2] = tin[1]
            send_t(2, to_last, 1).start()

        e = parts_of(tin.at[1])
        e = pick(joins, join(e, parts_of(tin.at[0])), e)

        @pl.when(chip == 3)
        def _():
            put(tout.at[2], join(e, parts_of(mown)))
            send_t(2, to_last, 1).start()
            back_t().start()

        enter_rows_of(e[1:3])
        pieces(last_step, 0, SCORES_AT)

    pass_rows(1 - core).wait_recv()
    entering = jnp.concatenate(
        [jnp.concatenate([vent[h, 0], vent[h, 1]], axis=1) for h in range(2)], axis=0
    )
    local_rows = jnp.zeros((head_rows, tokens), F32)
    for t in range(tiles):
        weight = jnp.broadcast_to(rd[t : t + 1, :], (head_rows, LANES)).astype(BF16)
        local_rows = local_rows + mm_nt(weight, y[t].astype(BF16))
    row_scores = []
    for s in range(spans):
        if s > 0:
            entering = enter_rows[0][:, SPAN - 1 : SPAN] * entering + read_states[0]
        far = mm_nt(entering.astype(BF16), c_ref[0, pl.ds(s * SPAN, SPAN), :]) * enter_rows[s]
        far = jnp.sum(far, axis=0, keepdims=True)
        row_scores.append(far + local_rows[0:1, s * SPAN : (s + 1) * SPAN])
    row_scores = jnp.where(live_row, jnp.concatenate(row_scores, axis=1), 0.0)
    for i in range(tokens // LANES):
        sums[mine, i : i + 1, :] = row_scores[:, i * LANES : (i + 1) * LANES]

    def score_copy(k):
        return pltpu.make_async_remote_copy(
            src_ref=sums.at[mine],
            dst_ref=sums.at[mine],
            send_sem=ysem_s.at[k],
            recv_sem=ysem_r.at[k],
            device_id={"head": lax.rem(mine + k, heads_axis)},
            device_id_type=MESH,
        )

    for k in range(1, heads_axis):
        score_copy(k).start()

    @pl.when(chip == 1)
    def _():
        for run in rest:
            run()

    @pl.when(chip >= 2)
    def _():
        pieces(last_step, SCORES_AT, half * steps)

    def finish_tile(t):
        cols = pl.ds(pl.multiple_of(t * LANES, LANES), LANES)
        e0 = eown[t]
        e1 = (ta[t][0:1, :] * e0.astype(F32) + first[t]).astype(BF16)
        for s, e in enumerate((e0, e1)):
            rows = pl.ds(s * SPAN, SPAN)
            enter = jnp.where(doc[rows, :] == 0.0, jnp.exp2(cum[t, rows, :]), 0.0)
            v = y[t, rows, :] + enter * mm(c_ref[0, rows, :], e)
            v = jnp.where(live[s * SPAN : (s + 1) * SPAN, :], v, 0.0).astype(BF16)
            out_ref[0, rows, cols] = v

    for j in range(half):
        finish_tile(core * half + j)
    for j in range(half):
        for r in range(steps):
            piece = pl.ds(r * ROWS_STEP, ROWS_STEP)
            pltpu.make_async_remote_copy(
                src_ref=psnd.at[j, piece],
                dst_ref=eown.at[(1 - core) * half + j, piece],
                send_sem=fsem_s.at[j, r],
                recv_sem=fsem_r.at[j, r],
                device_id={"ctx": partner},
                device_id_type=MESH,
            ).wait_recv()
        finish_tile((1 - core) * half + j)

    for k in range(1, heads_axis):
        score_copy(k).wait()
    total = sums[0]
    for k in range(1, heads_axis):
        total = total + sums[k]
    for i in range(tokens // LANES):
        score_ref[:, i * LANES : (i + 1) * LANES] = total[i : i + 1, :]

    for j in range(half):
        state_copy(sbf, srecv, psem_s, psem_r, j, partner).wait_send()
    t_copy.wait_send()
    pieces(lambda j, r: pass_copy(j, r).wait_send())

    @pl.when(among(0, 2, 3, 4))
    def _():
        send_t(0, to_lead, 0).wait_send()
        pieces(lambda j, r: send(outb.at[0], 0, j, r, to_lead, 0).wait_send())

    pass_rows(core).wait_send()

    @pl.when(among(1, 2, 5, 6))
    def _():
        send_t(1, to_join, join_slot).wait_send()
        pieces(lambda j, r: send(outb.at[1], 1, j, r, to_join, join_slot).wait_send())

    @pl.when(among(1, 3, 4, 7))
    def _():
        send_t(2, to_last, 1).wait_send()
        pieces(lambda j, r: send(outb.at[2], 2, j, r, to_last, 1).wait_send(), 0, half * steps - DIRECT)

    @pl.when(among(1, 3))
    def _():
        for out in (2, 3):
            pieces(
                lambda j, r: send(outb.at[2], out, j, r, 5, 1).wait_send(),
                half * steps - DIRECT,
                half * steps,
            )

    @pl.when(chip == 3)
    def _():
        back_t().wait_send()
        pieces(lambda j, r: send(inb.at[1], 4, j, r, 2, 1).wait_send())


def state_copy(src, dst, send, recv, j, partner):
    return pltpu.make_async_remote_copy(
        src_ref=src.at[j],
        dst_ref=dst.at[j],
        send_sem=send.at[j],
        recv_sem=recv.at[j],
        device_id={"ctx": partner},
        device_id_type=MESH,
    )


def body(inputs, b_proj, c_proj, log_decay, starts, counts, skip_gain, readout):
    tokens, width = inputs.shape[1:]
    ctxs, heads_axis = lax.axis_size("ctx"), lax.axis_size("head")
    tiles = width // LANES
    half = tiles // 2
    spans = tokens // SPAN
    steps = SPAN // ROWS_STEP
    vmem, smem = pl.BlockSpec(memory_space=pltpu.VMEM), pl.BlockSpec(memory_space=pltpu.SMEM)
    hbm = pl.BlockSpec(memory_space=pltpu.HBM)
    big = lambda n, dtype: pltpu.VMEM((n, SPAN, LANES), dtype)
    small = lambda n: pltpu.VMEM((n, 8, LANES), F32)
    sem = pltpu.SemaphoreType.DMA
    return pl.pallas_call(
        functools.partial(kernel, (ctxs, heads_axis, tokens, tiles)),
        out_shape=(
            jax.ShapeDtypeStruct(inputs.shape, BF16),
            jax.ShapeDtypeStruct((1, tokens), F32),
        ),
        in_specs=[smem, hbm, hbm, hbm, hbm, hbm, smem, hbm],
        out_specs=(vmem, vmem),
        scratch_shapes=[
            pltpu.VMEM(inputs.shape, BF16),
            pltpu.VMEM(b_proj.shape, BF16),
            pltpu.VMEM(c_proj.shape, BF16),
            pltpu.VMEM(log_decay.shape, BF16),
            pltpu.VMEM(starts.shape, starts.dtype),
            pltpu.VMEM((tiles, LANES), BF16),
            sem((6,)),
            pltpu.VMEM((tiles, tokens, LANES), BF16),
            pltpu.VMEM((tokens, width), BF16),
            pltpu.VMEM((tiles, tokens, LANES), F32),
            pltpu.VMEM((tokens, LANES), F32),
            pltpu.VMEM((SPAN, tokens), BF16),
            big(tiles, F32),
            big(tiles, F32),
            small(tiles),
            small(tiles),
            big(half, BF16),
            big(half, BF16),
            pltpu.VMEM((2, 4, 8, LANES), F32),
            small(4),
            small(4),
            big(half, F32),
            big(half, F32),
            small(4),
            small(4),
            pltpu.VMEM((2, half, SPAN, LANES), BF16),
            pltpu.VMEM((2, 4, 8, LANES), F32),
            pltpu.VMEM((3, half, SPAN, LANES), BF16),
            pltpu.VMEM((3, 4, 8, LANES), F32),
            big(tiles, BF16),
            big(half, BF16),
            pltpu.VMEM((2, 2, 8, LANES), F32),
            small(2),
            pltpu.VMEM((tiles, tokens, LANES), F32),
            pltpu.VMEM((spans, SPAN, SPAN), BF16),
            pltpu.VMEM((tokens // SUB, SUB, LANES), F32),
            pltpu.VMEM((heads_axis, tokens // LANES, LANES), F32),
            pltpu.VMEM((tiles, LANES), F32),
            sem((half,)), sem((half,)), sem((2,)),
            sem((5, half, steps)), sem((2, half, steps)), sem((4,)), sem((2,)),
            sem((half, steps)), sem((half, steps)), sem((2,)),
            sem((heads_axis,)), sem((heads_axis,)),
        ],
        compiler_params=pltpu.CompilerParams(collective_id=0, has_side_effects=True),
        name="ssd",
    )(counts, inputs, b_proj, c_proj, log_decay, starts, skip_gain, readout.reshape(tiles, LANES))


def solution(mesh):
    placed = (
        P("rep", "ctx", "head"),
        P("rep", "ctx", "head"),
        P("rep", "ctx", "head"),
        P("rep", "head", "ctx"),
        P("rep", "ctx"),
        P("rep", "ctx"),
        P("head"),
        P("head"),
    )
    return jax.shard_map(
        body,
        mesh=mesh,
        in_specs=placed,
        out_specs=(P("rep", "ctx", "head"), P("rep", "ctx")),
        check_vma=False,
    )
```

```python
import functools
import math

import jax
import jax.numpy as jnp
from jax import lax
from jax.experimental import pallas as pl
from jax.experimental.pallas import tpu as pltpu
from jax.sharding import PartitionSpec as P

SPAN = 256
HALF = 128
SUB = 64
LANES = 128
ROWS_STEP = 64
SCORES_AT = 6
DIRECT = 4
EDGES = ((0, 1), (1, 2), (2, 3), (1, 3), (1, 6), (1, 7), (3, 4), (3, 5), (4, 5), (5, 6), (6, 7))
LOG2E = math.log2(math.e)
F32 = jnp.float32
BF16 = jnp.bfloat16
MESH = pl.DeviceIdType.MESH


def mm(a, b):
    return lax.dot_general(a, b, (((1,), (0,)), ((), ())), preferred_element_type=F32)


def mm_nt(a, b):
    return lax.dot_general(a, b, (((1,), (1,)), ((), ())), preferred_element_type=F32)


def mm_tn(a, b):
    return lax.dot_general(a, b, (((0,), (0,)), ((), ())), preferred_element_type=F32)


def iota(shape, dim):
    return lax.broadcasted_iota(jnp.int32, shape, dim)


def kernel(
    sizes,
    count_ref, x_hbm, b_hbm, c_hbm, a_hbm, s_hbm, gain_ref, read_hbm,
    out_hbm, score_ref,
    out_ref, osem,
    x_ref, b_ref, c_ref, a_ref, s_ref, read_ref, isem,
    xm, lx, cum, doc, bt, first, whole, ta, td, sbf, srecv, mfull, msnd, mrecv,
    comb, base, mown, mbase, inb, tin, outb, tout, eown, psnd, vent, vsnd, y, gb, gm, sums, rd,
    psem_s, psem_r, tsem, csem_s, csem_r, vsem_s, vsem_r, fsem_s, fsem_r, wsem, ready, yready, ysem_s, ysem_r,
):
    ctxs, heads_axis, tokens, tiles = sizes
    half = tiles // 2
    spans = tokens // SPAN
    steps = SPAN // ROWS_STEP
    ctx = lax.axis_index("ctx")
    core = lax.rem(ctx, 2)
    chip = ctx // 2
    mine = lax.axis_index("head")
    partner = ctx + 1 - 2 * core

    loads = [
        pltpu.make_async_copy(source, target, isem.at[i])
        for i, (source, target) in enumerate(
            ((a_hbm, a_ref), (s_hbm, s_ref), (read_hbm, read_ref), (b_hbm, b_ref), (x_hbm, x_ref), (c_hbm, c_ref))
        )
    ]
    for load in loads:
        load.start()
    barrier = pltpu.get_barrier_semaphore()
    middle = heads_axis // 2

    def rank(i):
        return jnp.where(i < middle, i, heads_axis + middle - 1 - i)

    others = [lax.rem(mine + k, heads_axis) for k in range(heads_axis)]
    pl.semaphore_signal(barrier, inc=1, device_id={"ctx": partner}, device_id_type=MESH)
    peers = 1 + rank(mine)
    for here, there in EDGES:
        peers = peers + jnp.where(chip == there, 1, 0)

        @pl.when(chip == here)
        def _():
            pl.semaphore_signal(
                barrier, inc=1, device_id={"ctx": 2 * there + core}, device_id_type=MESH
            )

    for other in others[1:]:
        @pl.when(rank(other) > rank(mine))
        def _():
            pl.semaphore_signal(barrier, inc=1, device_id={"head": other}, device_id_type=MESH)

    count = count_ref[0, 0]
    live_row = iota((1, tokens), 1) < count
    loads[0].wait()
    loads[1].wait()
    log_decay = jnp.where(live_row, a_ref[0].astype(F32), 0.0).astype(BF16)
    starts = jnp.where(live_row, s_ref[...].astype(F32), 0.0)
    head_rows = log_decay.shape[0]
    all_starts = jnp.broadcast_to(starts, (head_rows, tokens)).astype(BF16)
    starts = jnp.where(iota((head_rows, tokens), 0) == 0, starts, 0.0).astype(BF16)
    spread = (iota((head_rows, tiles * LANES), 0) == iota((head_rows, tiles * LANES), 1) // SUB)
    spread = jnp.where(spread, 1.0, 0.0).astype(BF16)
    ones = jnp.ones((head_rows, LANES), BF16)
    tri = jnp.where(iota((SPAN, SPAN), 0) >= iota((SPAN, SPAN), 1), 1.0, 0.0).astype(BF16)
    for s in range(spans):
        rows = pl.ds(s * SPAN, SPAN)
        lx[rows, :] = mm_tn(log_decay[:, s * SPAN : (s + 1) * SPAN], spread).astype(BF16)
        spread_starts = mm_tn(starts[:, s * SPAN : (s + 1) * SPAN], ones).astype(BF16)
        doc[rows, :] = mm(tri, spread_starts)
    loads[3].wait()
    for s in range(spans):
        rows = pl.ds(s * SPAN, SPAN)
        bt[:, rows] = b_ref[0, rows, :].astype(F32).T.astype(BF16)
    loads[2].wait()
    loads[4].wait()

    live = iota((tokens, LANES), 0) < count

    pl.semaphore_wait(barrier, peers)
    for here, there in EDGES:
        if (here, there) != (1, 2):
            @pl.when(chip == there)
            def _():
                pl.semaphore_signal(
                    ready.at[there], inc=1, device_id={"ctx": 2 * here + core}, device_id_type=MESH
                )

    for other in others[1:]:
        @pl.when(rank(other) < rank(mine))
        def _():
            pl.semaphore_signal(yready, inc=1, device_id={"head": other}, device_id_type=MESH)

    def meet(here, *there):
        @pl.when(chip == here)
        def _():
            for other in there:
                pl.semaphore_wait(ready.at[other], 1)

    rd[...] = read_ref[...].astype(F32)
    upper = jnp.where(iota((SPAN, SPAN), 0) <= iota((SPAN, SPAN), 1), 1.0, 0.0).astype(BF16)
    head_of = iota((head_rows, LANES), 1) // SUB
    read_rows = jnp.zeros((head_rows, tokens), F32)
    for t in range(tiles):
        part = jnp.where(iota((head_rows, LANES), 0) == 2 * t + head_of, rd[t : t + 1, :], 0.0)
        read_rows = read_rows + mm_nt(part.astype(BF16), x_ref[0, :, t * LANES : (t + 1) * LANES])
    read_rows = jnp.where(live_row, read_rows, 0.0)
    enter_rows, read_states, row_totals = [], [], []
    for s in range(spans):
        lanes = slice(s * SPAN, (s + 1) * SPAN)
        run = mm(log_decay[:, lanes], upper) * LOG2E
        docs = mm(all_starts[:, lanes], upper)
        enter_rows.append(jnp.where(docs == 0.0, jnp.exp2(run), 0.0))
        ends = slice(SPAN - 1, SPAN)
        keep = jnp.where(docs == docs[:, ends], jnp.exp2(run[:, ends] - run), 0.0)
        read_states.append(mm((read_rows[:, lanes] * keep).astype(BF16), b_ref[0, pl.ds(s * SPAN, SPAN), :]))
        row_totals.append(jnp.broadcast_to(enter_rows[s][:, ends], (head_rows, LANES)))
    read_state = enter_rows[1][:, SPAN - 1 : SPAN] * read_states[0] + read_states[1]
    for h in range(2):
        rows = slice(h * 8, (h + 1) * 8)
        for i in range(2):
            mfull[h, 1 + i] = read_state[rows, i * LANES : (i + 1) * LANES]
        mfull[h, 3] = row_totals[0][rows] * row_totals[1][rows]

    def state_tile(t):
        cols = pl.ds(pl.multiple_of(t * LANES, LANES), LANES)
        xt = jnp.where(live, x_ref[0, :, cols].astype(F32), 0.0).astype(BF16)
        xm[t] = xt
        states, totals = [], []
        for s in range(spans):
            rows = slice(s * SPAN, (s + 1) * SPAN)
            run = mm(tri, lx[pl.ds(s * SPAN, SPAN), cols]) * LOG2E
            cum[t, pl.ds(s * SPAN, SPAN), :] = run
            docs = doc[pl.ds(s * SPAN, SPAN), :]
            last = run[SPAN - 1 : SPAN, :]
            keep = jnp.where(docs == docs[SPAN - 1 : SPAN, :], jnp.exp2(last - run), 0.0)
            weighted = (xt[rows, :].astype(F32) * keep).astype(BF16)
            states.append(mm(bt[:, pl.ds(s * SPAN, SPAN)], weighted))
            totals.append(jnp.where(docs[SPAN - 1 : SPAN, :] == 0.0, jnp.exp2(last), 0.0))
        first[t] = states[0]
        joined = totals[1] * states[0] + states[1]
        whole[t] = joined
        ta[t] = jnp.broadcast_to(totals[0], (8, LANES))
        td[t] = jnp.broadcast_to(totals[0] * totals[1], (8, LANES))
        return joined

    for j in range(half):
        sbf[j] = state_tile((1 - core) * half + j).astype(BF16)
        state_copy(sbf, srecv, psem_s, psem_r, j, partner).start()
    t_copy = pltpu.make_async_remote_copy(
        src_ref=msnd,
        dst_ref=mrecv,
        send_sem=tsem.at[0],
        recv_sem=tsem.at[1],
        device_id={"ctx": partner},
        device_id_type=MESH,
    )
    msnd[...] = mfull[1 - core]
    for j in range(half):
        msnd[0, j : j + 1, :] = td[(1 - core) * half + j][0:1, :]
    t_copy.start()
    for j in range(half):
        state_tile(core * half + j)
        mfull[core, 0, j : j + 1, :] = td[core * half + j][0:1, :]

    def join(earlier, later):
        columns = later[3]
        return (
            later[0] * earlier[0],
            columns * earlier[1] + later[1],
            columns * earlier[2] + later[2],
            columns * earlier[3],
        )

    def put(ref, parts):
        for i, part in enumerate(parts):
            ref[i] = part

    def pick(choose, a, b):
        return tuple(jnp.where(choose, u, v) for u, v in zip(a, b))

    def parts_of(ref):
        return tuple(ref[i] for i in range(4))

    t_copy.wait_recv()
    is_low = core == 0
    own_parts, their_parts = parts_of(mfull.at[core]), parts_of(mrecv)
    low_parts, high_parts = pick(is_low, own_parts, their_parts), pick(is_low, their_parts, own_parts)
    put(mown, join(low_parts, high_parts))
    put(mbase, low_parts)
    for j in range(half):
        state_copy(sbf, srecv, psem_s, psem_r, j, partner).wait_recv()
        own, theirs = whole[core * half + j], srecv[j].astype(F32)
        low, high = jnp.where(is_low, own, theirs), jnp.where(is_low, theirs, own)
        comb[j] = high_parts[0][j : j + 1, :] * low + high
        base[j] = low

    def send(src, out, j, r, to, slot):
        piece = rows_of(r)
        return pltpu.make_async_remote_copy(
            src_ref=src.at[j, piece],
            dst_ref=inb.at[slot, j, piece],
            send_sem=csem_s.at[out, j, r],
            recv_sem=csem_r.at[slot, j, r],
            device_id={"ctx": 2 * to + core},
            device_id_type=MESH,
        )

    def send_t(out, to, slot):
        return pltpu.make_async_remote_copy(
            src_ref=tout.at[out],
            dst_ref=tin.at[slot],
            send_sem=vsem_s.at[out],
            recv_sem=vsem_r.at[slot],
            device_id={"ctx": 2 * to + core},
            device_id_type=MESH,
        )

    def back_t():
        return pltpu.make_async_remote_copy(
            src_ref=tin.at[1],
            dst_ref=tin.at[1],
            send_sem=vsem_s.at[3],
            recv_sem=vsem_r.at[1],
            device_id={"ctx": 4 + core},
            device_id_type=MESH,
        )

    def pieces(step, begin=0, end=half * steps):
        def one(q, _):
            step(q // steps, lax.rem(q, steps))
            return 0

        lax.fori_loop(begin, end, one, 0)

    def rows_of(r):
        return pl.ds(pl.multiple_of(r * ROWS_STEP, ROWS_STEP), ROWS_STEP)

    def of_chip(*values):
        result = values[-1]
        for i, value in enumerate(values[:-1]):
            result = jnp.where(chip == i, value, result)
        return result

    def among(*chips):
        return functools.reduce(jnp.logical_or, [chip == i for i in chips])

    to_lead = of_chip(1, 0, 3, 2, 5, 4, 4, 4)
    to_join = of_chip(1, 3, 1, 1, 4, 6, 7, 6)
    join_slot = jnp.where(chip < 3, 1, 0)
    to_last = of_chip(1, 7, 1, 4, 5, 4, 4, 6)

    def pass_copy(j, r):
        piece = rows_of(r)
        return pltpu.make_async_remote_copy(
            src_ref=psnd.at[j, piece],
            dst_ref=eown.at[core * half + j, piece],
            send_sem=fsem_s.at[j, r],
            recv_sem=fsem_r.at[j, r],
            device_id={"ctx": partner},
            device_id_type=MESH,
        )

    def local_part():
        loads[5].wait()
        for s in range(spans):
            rows = pl.ds(s * SPAN, SPAN)
            scores = mm_nt(c_ref[0, rows, :], b_ref[0, rows, :])
            gb[s] = scores.astype(BF16)
        lane = iota((SUB, LANES), 1)
        lane = jnp.where(lane < SUB, lane, lane - SUB)
        row = iota((SUB, LANES), 0)
        eye = jnp.where(row == lane, 1.0, 0.0)
        for k in range(tokens // SUB):
            rows = pl.ds(k * SUB, SUB)
            bk = b_ref[0, rows, :]
            sc = mm_nt(c_ref[0, rows, :], jnp.concatenate([bk, bk], axis=0))
            dk = doc[rows, :]
            drow = jnp.sum(dk * eye, axis=0, keepdims=True)
            gm[k] = jnp.where((row >= lane) & (dk == drow), sc, 0.0)
        low_lane = iota((SUB, LANES), 1) < SUB
        one_lane = iota((1, LANES), 1) < SUB

        def tile(t, _):
            skip = jnp.where(one_lane, gain_ref[2 * t], gain_ref[2 * t + 1])
            for s in range(spans):
                o = s * SPAN

                def level(at, width):
                    lo, hi = pl.ds(o + at, width), pl.ds(o + at + width, width)
                    run_lo, run_hi = cum[t, lo, :], cum[t, hi, :]
                    doc_lo, doc_hi = doc[lo, :], doc[hi, :]
                    ref, ref_doc = run_lo[width - 1 : width, :], doc_lo[width - 1 : width, :]
                    keep = jnp.where(doc_lo == ref_doc, jnp.exp2(ref - run_lo), 0.0)
                    enter = jnp.where(doc_hi == ref_doc, jnp.exp2(run_hi - ref), 0.0)
                    weighted = (xm[t, lo, :].astype(F32) * keep).astype(BF16)
                    part = gb[s, at + width : at + 2 * width, at : at + width]
                    return enter * mm(part, weighted)

                far = level(0, HALF)
                near = [level(0, SUB), level(HALF, SUB)]
                for q in range(SPAN // SUB):
                    rows = pl.ds(o + q * SUB, SUB)
                    run = cum[t, rows, :]
                    xq = xm[t, rows, :]
                    xf = xq.astype(F32)
                    run_row = jnp.sum(run * eye, axis=0, keepdims=True)
                    w = jnp.exp2(jnp.minimum(run - run_row, 0.0)) * gm[s * (SPAN // SUB) + q]
                    left = jnp.where(low_lane, xf, 0.0).astype(BF16)
                    right = jnp.where(low_lane, 0.0, xf).astype(BF16)
                    v = mm(w.astype(BF16), jnp.concatenate([left, right], axis=0))
                    v = v + skip * xf
                    if q % 2 == 1:
                        v = v + near[q // 2]
                    if q >= 2:
                        v = v + far[(q - 2) * SUB : (q - 1) * SUB, :]
                    y[t, rows, :] = v
            return 0

        lax.fori_loop(0, tiles, tile, 0)

    meet(0, 1)
    meet(2, 3)
    meet(4, 5)

    @pl.when(among(0, 2, 3, 4))
    def _():
        tout[0] = mown[...]
        send_t(0, to_lead, 0).start()

        def step(j, r):
            piece = rows_of(r)
            outb[0, j, piece, :] = comb[j, piece, :].astype(BF16)
            send(outb.at[0], 0, j, r, to_lead, 0).start()

        pieces(step)

    local_part()
    meet(1, 3)
    meet(5, 6)
    meet(6, 7)

    @pl.when(among(1, 2, 3, 5, 6, 7))
    def _():
        send_t(0, to_lead, 0).wait_recv()

    def row(ref, j):
        return ref[0, pl.ds(j, 1), :]

    is_later = chip == 2

    @pl.when(among(1, 2, 5, 6))
    def _():
        got, own = parts_of(tin.at[0]), parts_of(mown)
        put(tout.at[1], join(pick(is_later, own, got), pick(is_later, got, own)))
        send_t(1, to_join, join_slot).start()

    def enter(j, r, e):
        piece = rows_of(r)
        f = row(mbase, j) * e + base[j, piece, :]
        eown[core * half + j, piece, :] = jnp.where(is_low, e, f).astype(BF16)
        psnd[j, piece, :] = jnp.where(is_low, f, e).astype(BF16)
        pass_copy(j, r).start()

    def join_step(j, r):
        piece = rows_of(r)
        send(outb.at[0], 0, j, r, to_lead, 0).wait_recv()
        got, own = inb[0, j, piece, :].astype(F32), comb[j, piece, :]
        scale = jnp.where(is_later, row(tin.at[0], j), row(mown, j))
        joined = scale * jnp.where(is_later, own, got) + jnp.where(is_later, got, own)
        outb[1, j, piece, :] = joined.astype(BF16)
        send(outb.at[1], 1, j, r, to_join, join_slot).start()

        @pl.when(chip == 1)
        def _():
            enter(j, r, got)

    @pl.when(among(2, 5, 6))
    def _():
        pieces(join_step)

    def pass_rows(side):
        return pltpu.make_async_remote_copy(
            src_ref=vsnd,
            dst_ref=vent.at[side],
            send_sem=wsem.at[0],
            recv_sem=wsem.at[1],
            device_id={"ctx": partner},
            device_id_type=MESH,
        )

    def enter_rows_of(e):
        for i in range(2):
            f = mbase[3] * e[i] + mbase[1 + i]
            vent[core, i] = jnp.where(is_low, e[i], f)
            vsnd[i] = jnp.where(is_low, f, e[i])
        pass_rows(core).start()

    @pl.when(chip == 0)
    def _():
        enter_rows_of((jnp.zeros((8, LANES), F32),) * 2)
        pieces(lambda j, r: enter(j, r, jnp.zeros((ROWS_STEP, LANES), F32)))

    def direct(j, r, to):
        @pl.when(j * steps + r >= half * steps - DIRECT)
        def _():
            send(outb.at[2], 3, j, r, to, 1).start()

    rest = []

    @pl.when(chip == 1)
    def _():
        enter_rows_of((tin[0, 1], tin[0, 2]))

        def last_step(j, r):
            piece = rows_of(r)
            send(outb.at[1], 1, j, r, 1, 1).wait_recv()
            got, own = inb[1, j, piece, :].astype(F32), outb[1, j, piece, :].astype(F32)
            outb[2, j, piece, :] = (row(tin.at[1], j) * own + got).astype(BF16)
            send(outb.at[2], 2, j, r, 7, 1).start()
            direct(j, r, 6)

        def both(j, r):
            join_step(j, r)
            last_step(j - behind // steps, r)

        behind = (half // 2) * steps
        pieces(join_step, 0, behind)
        send_t(1, 1, 1).wait_recv()
        meet(1, 6, 7)
        put(tout.at[2], join(parts_of(tout.at[1]), parts_of(tin.at[1])))
        send_t(2, 7, 1).start()
        pieces(both, behind, half * steps)
        rest.append(lambda: pieces(last_step, half * steps - behind, half * steps))

    joins = among(3, 5, 6, 7)

    def last_step(j, r):
        piece = rows_of(r)
        send(outb.at[2], 2, j, r, 1, 1).wait_recv()

        @pl.when(among(4, 7) & (j * steps + r < half * steps - DIRECT))
        def _():
            send(inb.at[1], 2, j, r, to_last, 1).start()

        @pl.when(among(3, 7))
        def _():
            send(outb.at[0], 0, j, r, to_lead, 0).wait_recv()

        got = inb[1, j, piece, :].astype(F32)
        add = jnp.where(joins, inb[0, j, piece, :].astype(F32), 0.0)
        e = jnp.where(joins, row(tin.at[0], j), 1.0) * got + add

        @pl.when(chip == 3)
        def _():
            outb[2, j, piece, :] = (row(mown, j) * e + comb[j, piece, :]).astype(BF16)
            send(outb.at[2], 2, j, r, 4, 1).start()
            direct(j, r, 5)
            send(inb.at[1], 4, j, r, 2, 1).start()

        enter(j, r, e)

    @pl.when(chip >= 2)
    def _():
        send_t(2, 1, 1).wait_recv()
        meet(3, 4, 5)

        @pl.when(among(4, 7))
        def _():
            tout[2] = tin[1]
            send_t(2, to_last, 1).start()

        e = parts_of(tin.at[1])
        e = pick(joins, join(e, parts_of(tin.at[0])), e)

        @pl.when(chip == 3)
        def _():
            put(tout.at[2], join(e, parts_of(mown)))
            send_t(2, to_last, 1).start()
            back_t().start()

        enter_rows_of(e[1:3])
        pieces(last_step, 0, SCORES_AT)

    pass_rows(1 - core).wait_recv()
    entering = jnp.concatenate(
        [jnp.concatenate([vent[h, 0], vent[h, 1]], axis=1) for h in range(2)], axis=0
    )
    local_rows = jnp.zeros((head_rows, tokens), F32)
    for t in range(tiles):
        weight = jnp.broadcast_to(rd[t : t + 1, :], (head_rows, LANES)).astype(BF16)
        local_rows = local_rows + mm_nt(weight, y[t].astype(BF16))
    row_scores = []
    for s in range(spans):
        if s > 0:
            entering = enter_rows[0][:, SPAN - 1 : SPAN] * entering + read_states[0]
        far = mm_nt(entering.astype(BF16), c_ref[0, pl.ds(s * SPAN, SPAN), :]) * enter_rows[s]
        far = jnp.sum(far, axis=0, keepdims=True)
        row_scores.append(far + local_rows[0:1, s * SPAN : (s + 1) * SPAN])
    row_scores = jnp.where(live_row, jnp.concatenate(row_scores, axis=1), 0.0)
    for i in range(tokens // LANES):
        sums[mine, i : i + 1, :] = row_scores[:, i * LANES : (i + 1) * LANES]

    def score_copy(k):
        return pltpu.make_async_remote_copy(
            src_ref=sums.at[mine],
            dst_ref=sums.at[mine],
            send_sem=ysem_s.at[k],
            recv_sem=ysem_r.at[k],
            device_id={"head": lax.rem(mine + k, heads_axis)},
            device_id_type=MESH,
        )

    @pl.when(rank(mine) < heads_axis - 1)
    def _():
        pl.semaphore_wait(yready, heads_axis - 1 - rank(mine))

    for k in range(1, heads_axis):
        score_copy(k).start()

    @pl.when(chip == 1)
    def _():
        for run in rest:
            run()

    @pl.when(chip >= 2)
    def _():
        pieces(last_step, SCORES_AT, half * steps)

    def out_copy(t):
        return pltpu.make_async_copy(
            out_ref.at[t],
            out_hbm.at[0, :, pl.ds(pl.multiple_of(t * LANES, LANES), LANES)],
            osem.at[t],
        )

    def finish_tile(t):
        cols = pl.ds(pl.multiple_of(t * LANES, LANES), LANES)
        e0 = eown[t]
        e1 = (ta[t][0:1, :] * e0.astype(F32) + first[t]).astype(BF16)
        for s, e in enumerate((e0, e1)):
            rows = pl.ds(s * SPAN, SPAN)
            enter = jnp.where(doc[rows, :] == 0.0, jnp.exp2(cum[t, rows, :]), 0.0)
            v = y[t, rows, :] + enter * mm(c_ref[0, rows, :], e)
            v = jnp.where(live[s * SPAN : (s + 1) * SPAN, :], v, 0.0).astype(BF16)
            out_ref[t, rows, :] = v
        out_copy(t).start()

    for j in range(half):
        finish_tile(core * half + j)
    for j in range(half):
        for r in range(steps):
            piece = pl.ds(r * ROWS_STEP, ROWS_STEP)
            pltpu.make_async_remote_copy(
                src_ref=psnd.at[j, piece],
                dst_ref=eown.at[(1 - core) * half + j, piece],
                send_sem=fsem_s.at[j, r],
                recv_sem=fsem_r.at[j, r],
                device_id={"ctx": partner},
                device_id_type=MESH,
            ).wait_recv()
        finish_tile((1 - core) * half + j)

    for k in range(1, heads_axis):
        score_copy(k).wait()
    total = sums[0]
    for k in range(1, heads_axis):
        total = total + sums[k]
    for i in range(tokens // LANES):
        score_ref[:, i * LANES : (i + 1) * LANES] = total[i : i + 1, :]

    for t in range(tiles):
        out_copy(t).wait()
    for j in range(half):
        state_copy(sbf, srecv, psem_s, psem_r, j, partner).wait_send()
    t_copy.wait_send()
    pieces(lambda j, r: pass_copy(j, r).wait_send())

    @pl.when(among(0, 2, 3, 4))
    def _():
        send_t(0, to_lead, 0).wait_send()
        pieces(lambda j, r: send(outb.at[0], 0, j, r, to_lead, 0).wait_send())

    pass_rows(core).wait_send()

    @pl.when(among(1, 2, 5, 6))
    def _():
        send_t(1, to_join, join_slot).wait_send()
        pieces(lambda j, r: send(outb.at[1], 1, j, r, to_join, join_slot).wait_send())

    @pl.when(among(1, 3, 4, 7))
    def _():
        send_t(2, to_last, 1).wait_send()
        pieces(lambda j, r: send(outb.at[2], 2, j, r, to_last, 1).wait_send(), 0, half * steps - DIRECT)

    @pl.when(among(1, 3))
    def _():
        for out in (2, 3):
            pieces(
                lambda j, r: send(outb.at[2], out, j, r, 5, 1).wait_send(),
                half * steps - DIRECT,
                half * steps,
            )

    @pl.when(chip == 3)
    def _():
        back_t().wait_send()
        pieces(lambda j, r: send(inb.at[1], 4, j, r, 2, 1).wait_send())


def state_copy(src, dst, send, recv, j, partner):
    return pltpu.make_async_remote_copy(
        src_ref=src.at[j],
        dst_ref=dst.at[j],
        send_sem=send.at[j],
        recv_sem=recv.at[j],
        device_id={"ctx": partner},
        device_id_type=MESH,
    )


def body(inputs, b_proj, c_proj, log_decay, starts, counts, skip_gain, readout):
    tokens, width = inputs.shape[1:]
    ctxs, heads_axis = lax.axis_size("ctx"), lax.axis_size("head")
    tiles = width // LANES
    half = tiles // 2
    spans = tokens // SPAN
    steps = SPAN // ROWS_STEP
    vmem, smem = pl.BlockSpec(memory_space=pltpu.VMEM), pl.BlockSpec(memory_space=pltpu.SMEM)
    hbm = pl.BlockSpec(memory_space=pltpu.HBM)
    big = lambda n, dtype: pltpu.VMEM((n, SPAN, LANES), dtype)
    small = lambda n: pltpu.VMEM((n, 8, LANES), F32)
    sem = pltpu.SemaphoreType.DMA
    return pl.pallas_call(
        functools.partial(kernel, (ctxs, heads_axis, tokens, tiles)),
        out_shape=(
            jax.ShapeDtypeStruct(inputs.shape, BF16),
            jax.ShapeDtypeStruct((1, tokens), F32),
        ),
        in_specs=[smem, hbm, hbm, hbm, hbm, hbm, smem, hbm],
        out_specs=(pl.BlockSpec(memory_space=pltpu.HBM), vmem),
        scratch_shapes=[
            pltpu.VMEM((tiles, tokens, LANES), BF16),
            sem((tiles,)),
            pltpu.VMEM(inputs.shape, BF16),
            pltpu.VMEM(b_proj.shape, BF16),
            pltpu.VMEM(c_proj.shape, BF16),
            pltpu.VMEM(log_decay.shape, BF16),
            pltpu.VMEM(starts.shape, starts.dtype),
            pltpu.VMEM((tiles, LANES), BF16),
            sem((6,)),
            pltpu.VMEM((tiles, tokens, LANES), BF16),
            pltpu.VMEM((tokens, width), BF16),
            pltpu.VMEM((tiles, tokens, LANES), F32),
            pltpu.VMEM((tokens, LANES), F32),
            pltpu.VMEM((SPAN, tokens), BF16),
            big(tiles, F32),
            big(tiles, F32),
            small(tiles),
            small(tiles),
            big(half, BF16),
            big(half, BF16),
            pltpu.VMEM((2, 4, 8, LANES), F32),
            small(4),
            small(4),
            big(half, F32),
            big(half, F32),
            small(4),
            small(4),
            pltpu.VMEM((2, half, SPAN, LANES), BF16),
            pltpu.VMEM((2, 4, 8, LANES), F32),
            pltpu.VMEM((3, half, SPAN, LANES), BF16),
            pltpu.VMEM((3, 4, 8, LANES), F32),
            big(tiles, BF16),
            big(half, BF16),
            pltpu.VMEM((2, 2, 8, LANES), F32),
            small(2),
            pltpu.VMEM((tiles, tokens, LANES), F32),
            pltpu.VMEM((spans, SPAN, SPAN), BF16),
            pltpu.VMEM((tokens // SUB, SUB, LANES), F32),
            pltpu.VMEM((heads_axis, tokens // LANES, LANES), F32),
            pltpu.VMEM((tiles, LANES), F32),
            sem((half,)), sem((half,)), sem((2,)),
            sem((5, half, steps)), sem((2, half, steps)), sem((4,)), sem((2,)),
            sem((half, steps)), sem((half, steps)), sem((2,)),
            pltpu.SemaphoreType.REGULAR((ctxs // 2,)), pltpu.SemaphoreType.REGULAR,
            sem((heads_axis,)), sem((heads_axis,)),
        ],
        compiler_params=pltpu.CompilerParams(collective_id=0, has_side_effects=True),
        name="ssd",
    )(counts, inputs, b_proj, c_proj, log_decay, starts, skip_gain, readout.reshape(tiles, LANES))


def solution(mesh):
    placed = (
        P("rep", "ctx", "head"),
        P("rep", "ctx", "head"),
        P("rep", "ctx", "head"),
        P("rep", "head", "ctx"),
        P("rep", "ctx"),
        P("rep", "ctx"),
        P("head"),
        P("head"),
    )
    return jax.shard_map(
        body,
        mesh=mesh,
        in_specs=placed,
        out_specs=(P("rep", "ctx", "head"), P("rep", "ctx")),
        check_vma=False,
    )
```

```python
import functools
import math

import jax
import jax.numpy as jnp
from jax import lax
from jax.experimental import pallas as pl
from jax.experimental.pallas import tpu as pltpu
from jax.sharding import PartitionSpec as P

SPAN = 256
HALF = 128
SUB = 64
LANES = 128
ROWS_STEP = 64
SCORES_AT = 3
DIRECT = 6
EDGES = ((0, 1), (1, 2), (2, 3), (1, 3), (1, 6), (1, 7), (3, 4), (3, 5), (4, 5), (5, 6), (6, 7))
LOG2E = math.log2(math.e)
F32 = jnp.float32
BF16 = jnp.bfloat16
MESH = pl.DeviceIdType.MESH


def mm(a, b):
    return lax.dot_general(a, b, (((1,), (0,)), ((), ())), preferred_element_type=F32)


def mm_nt(a, b):
    return lax.dot_general(a, b, (((1,), (1,)), ((), ())), preferred_element_type=F32)


def mm_tn(a, b):
    return lax.dot_general(a, b, (((0,), (0,)), ((), ())), preferred_element_type=F32)


def iota(shape, dim):
    return lax.broadcasted_iota(jnp.int32, shape, dim)


def kernel(
    sizes,
    count_ref, x_hbm, b_hbm, c_hbm, a_hbm, s_hbm, gain_ref, read_hbm,
    out_hbm, score_ref,
    out_ref, osem,
    x_ref, b_ref, c_ref, a_ref, s_ref, read_ref, isem,
    xm, lx, cum, doc, bt, first, whole, ta, td, sbf, srecv, mfull, msnd, mrecv,
    comb, base, mown, mbase, inb, tin, outb, tout, eown, psnd, vent, vsnd, y, gb, gm, sums, rd,
    psem_s, psem_r, tsem, csem_s, csem_r, vsem_s, vsem_r, fsem_s, fsem_r, wsem, ready, yready, ysem_s, ysem_r,
):
    ctxs, heads_axis, tokens, tiles = sizes
    half = tiles // 2
    spans = tokens // SPAN
    steps = SPAN // ROWS_STEP
    ctx = lax.axis_index("ctx")
    core = lax.rem(ctx, 2)
    chip = ctx // 2
    mine = lax.axis_index("head")
    partner = ctx + 1 - 2 * core

    loads = [
        pltpu.make_async_copy(source, target, isem.at[i])
        for i, (source, target) in enumerate(
            ((a_hbm, a_ref), (s_hbm, s_ref), (read_hbm, read_ref), (b_hbm, b_ref), (x_hbm, x_ref), (c_hbm, c_ref))
        )
    ]
    for load in loads:
        load.start()
    barrier = pltpu.get_barrier_semaphore()
    middle = heads_axis // 2

    def rank(i):
        return jnp.where(i < middle, i, heads_axis + middle - 1 - i)

    others = [lax.rem(mine + k, heads_axis) for k in range(heads_axis)]
    pl.semaphore_signal(barrier, inc=1, device_id={"ctx": partner}, device_id_type=MESH)
    peers = 1 + rank(mine)
    for here, there in EDGES:
        peers = peers + jnp.where(chip == there, 1, 0)

        @pl.when(chip == here)
        def _():
            pl.semaphore_signal(
                barrier, inc=1, device_id={"ctx": 2 * there + core}, device_id_type=MESH
            )

    for other in others[1:]:
        @pl.when(rank(other) > rank(mine))
        def _():
            pl.semaphore_signal(barrier, inc=1, device_id={"head": other}, device_id_type=MESH)

    count = count_ref[0, 0]
    live_row = iota((1, tokens), 1) < count
    loads[0].wait()
    loads[1].wait()
    log_decay = jnp.where(live_row, a_ref[0].astype(F32), 0.0).astype(BF16)
    starts = jnp.where(live_row, s_ref[...].astype(F32), 0.0)
    head_rows = log_decay.shape[0]
    all_starts = jnp.broadcast_to(starts, (head_rows, tokens)).astype(BF16)
    starts = jnp.where(iota((head_rows, tokens), 0) == 0, starts, 0.0).astype(BF16)
    spread = (iota((head_rows, tiles * LANES), 0) == iota((head_rows, tiles * LANES), 1) // SUB)
    spread = jnp.where(spread, 1.0, 0.0).astype(BF16)
    ones = jnp.ones((head_rows, LANES), BF16)
    tri = jnp.where(iota((SPAN, SPAN), 0) >= iota((SPAN, SPAN), 1), 1.0, 0.0).astype(BF16)
    for s in range(spans):
        rows = pl.ds(s * SPAN, SPAN)
        lx[rows, :] = mm_tn(log_decay[:, s * SPAN : (s + 1) * SPAN], spread).astype(BF16)
        spread_starts = mm_tn(starts[:, s * SPAN : (s + 1) * SPAN], ones).astype(BF16)
        doc[rows, :] = mm(tri, spread_starts)
    loads[3].wait()
    for s in range(spans):
        rows = pl.ds(s * SPAN, SPAN)
        bt[:, rows] = b_ref[0, rows, :].astype(F32).T.astype(BF16)
    loads[2].wait()
    loads[4].wait()

    live = iota((tokens, LANES), 0) < count

    pl.semaphore_wait(barrier, peers)
    for here, there in EDGES:
        @pl.when(chip == there)
        def _():
            pl.semaphore_signal(
                ready.at[there], inc=1, device_id={"ctx": 2 * here + core}, device_id_type=MESH
            )

    for other in others[1:]:
        @pl.when(rank(other) < rank(mine))
        def _():
            pl.semaphore_signal(yready, inc=1, device_id={"head": other}, device_id_type=MESH)

    def meet(here, *there):
        @pl.when(chip == here)
        def _():
            for other in there:
                pl.semaphore_wait(ready.at[other], 1)

    rd[...] = read_ref[...].astype(F32)
    upper = jnp.where(iota((SPAN, SPAN), 0) <= iota((SPAN, SPAN), 1), 1.0, 0.0).astype(BF16)
    head_of = iota((head_rows, LANES), 1) // SUB
    read_rows = jnp.zeros((head_rows, tokens), F32)
    for t in range(tiles):
        part = jnp.where(iota((head_rows, LANES), 0) == 2 * t + head_of, rd[t : t + 1, :], 0.0)
        read_rows = read_rows + mm_nt(part.astype(BF16), x_ref[0, :, t * LANES : (t + 1) * LANES])
    read_rows = jnp.where(live_row, read_rows, 0.0)
    enter_rows, read_states, row_totals = [], [], []
    for s in range(spans):
        lanes = slice(s * SPAN, (s + 1) * SPAN)
        run = mm(log_decay[:, lanes], upper) * LOG2E
        docs = mm(all_starts[:, lanes], upper)
        enter_rows.append(jnp.where(docs == 0.0, jnp.exp2(run), 0.0))
        ends = slice(SPAN - 1, SPAN)
        keep = jnp.where(docs == docs[:, ends], jnp.exp2(run[:, ends] - run), 0.0)
        read_states.append(mm((read_rows[:, lanes] * keep).astype(BF16), b_ref[0, pl.ds(s * SPAN, SPAN), :]))
        row_totals.append(jnp.broadcast_to(enter_rows[s][:, ends], (head_rows, LANES)))
    read_state = enter_rows[1][:, SPAN - 1 : SPAN] * read_states[0] + read_states[1]
    for h in range(2):
        rows = slice(h * 8, (h + 1) * 8)
        for i in range(2):
            mfull[h, 1 + i] = read_state[rows, i * LANES : (i + 1) * LANES]
        mfull[h, 3] = row_totals[0][rows] * row_totals[1][rows]

    def state_tile(t):
        cols = pl.ds(pl.multiple_of(t * LANES, LANES), LANES)
        xt = jnp.where(live, x_ref[0, :, cols].astype(F32), 0.0).astype(BF16)
        xm[t] = xt
        states, totals = [], []
        for s in range(spans):
            rows = slice(s * SPAN, (s + 1) * SPAN)
            run = mm(tri, lx[pl.ds(s * SPAN, SPAN), cols]) * LOG2E
            cum[t, pl.ds(s * SPAN, SPAN), :] = run
            docs = doc[pl.ds(s * SPAN, SPAN), :]
            last = run[SPAN - 1 : SPAN, :]
            keep = jnp.where(docs == docs[SPAN - 1 : SPAN, :], jnp.exp2(last - run), 0.0)
            weighted = (xt[rows, :].astype(F32) * keep).astype(BF16)
            states.append(mm(bt[:, pl.ds(s * SPAN, SPAN)], weighted))
            totals.append(jnp.where(docs[SPAN - 1 : SPAN, :] == 0.0, jnp.exp2(last), 0.0))
        first[t] = states[0]
        joined = totals[1] * states[0] + states[1]
        whole[t] = joined
        ta[t] = jnp.broadcast_to(totals[0], (8, LANES))
        td[t] = jnp.broadcast_to(totals[0] * totals[1], (8, LANES))
        return joined

    for j in range(half):
        sbf[j] = state_tile((1 - core) * half + j).astype(BF16)
        state_copy(sbf, srecv, psem_s, psem_r, j, partner).start()
    t_copy = pltpu.make_async_remote_copy(
        src_ref=msnd,
        dst_ref=mrecv,
        send_sem=tsem.at[0],
        recv_sem=tsem.at[1],
        device_id={"ctx": partner},
        device_id_type=MESH,
    )
    msnd[...] = mfull[1 - core]
    for j in range(half):
        msnd[0, j : j + 1, :] = td[(1 - core) * half + j][0:1, :]
    t_copy.start()
    for j in range(half):
        state_tile(core * half + j)
        mfull[core, 0, j : j + 1, :] = td[core * half + j][0:1, :]

    def join(earlier, later):
        columns = later[3]
        return (
            later[0] * earlier[0],
            columns * earlier[1] + later[1],
            columns * earlier[2] + later[2],
            columns * earlier[3],
        )

    def put(ref, parts):
        for i, part in enumerate(parts):
            ref[i] = part

    def pick(choose, a, b):
        return tuple(jnp.where(choose, u, v) for u, v in zip(a, b))

    def parts_of(ref):
        return tuple(ref[i] for i in range(4))

    t_copy.wait_recv()
    is_low = core == 0
    own_parts, their_parts = parts_of(mfull.at[core]), parts_of(mrecv)
    low_parts, high_parts = pick(is_low, own_parts, their_parts), pick(is_low, their_parts, own_parts)
    put(mown, join(low_parts, high_parts))
    put(mbase, low_parts)
    for j in range(half):
        state_copy(sbf, srecv, psem_s, psem_r, j, partner).wait_recv()
        own, theirs = whole[core * half + j], srecv[j].astype(F32)
        low, high = jnp.where(is_low, own, theirs), jnp.where(is_low, theirs, own)
        comb[j] = high_parts[0][j : j + 1, :] * low + high
        base[j] = low

    def send(src, out, j, r, to, slot):
        piece = rows_of(r)
        return pltpu.make_async_remote_copy(
            src_ref=src.at[j, piece],
            dst_ref=inb.at[slot, j, piece],
            send_sem=csem_s.at[out, j, r],
            recv_sem=csem_r.at[slot, j, r],
            device_id={"ctx": 2 * to + core},
            device_id_type=MESH,
        )

    def send_t(out, to, slot):
        return pltpu.make_async_remote_copy(
            src_ref=tout.at[out],
            dst_ref=tin.at[slot],
            send_sem=vsem_s.at[out],
            recv_sem=vsem_r.at[slot],
            device_id={"ctx": 2 * to + core},
            device_id_type=MESH,
        )

    def back_t():
        return pltpu.make_async_remote_copy(
            src_ref=tin.at[1],
            dst_ref=tin.at[1],
            send_sem=vsem_s.at[3],
            recv_sem=vsem_r.at[1],
            device_id={"ctx": 4 + core},
            device_id_type=MESH,
        )

    def pieces(step, begin=0, end=half * steps):
        def one(q, _):
            step(q // steps, lax.rem(q, steps))
            return 0

        lax.fori_loop(begin, end, one, 0)

    def rows_of(r):
        return pl.ds(pl.multiple_of(r * ROWS_STEP, ROWS_STEP), ROWS_STEP)

    def of_chip(*values):
        result = values[-1]
        for i, value in enumerate(values[:-1]):
            result = jnp.where(chip == i, value, result)
        return result

    def among(*chips):
        return functools.reduce(jnp.logical_or, [chip == i for i in chips])

    to_lead = of_chip(1, 0, 3, 2, 5, 4, 4, 4)
    to_join = of_chip(1, 3, 1, 1, 4, 6, 7, 6)
    join_slot = jnp.where(chip < 3, 1, 0)
    to_last = of_chip(1, 7, 1, 4, 5, 4, 4, 6)

    def pass_copy(j, r):
        piece = rows_of(r)
        return pltpu.make_async_remote_copy(
            src_ref=psnd.at[j, piece],
            dst_ref=eown.at[core * half + j, piece],
            send_sem=fsem_s.at[j, r],
            recv_sem=fsem_r.at[j, r],
            device_id={"ctx": partner},
            device_id_type=MESH,
        )

    def local_part():
        loads[5].wait()
        for s in range(spans):
            rows = pl.ds(s * SPAN, SPAN)
            scores = mm_nt(c_ref[0, rows, :], b_ref[0, rows, :])
            gb[s] = scores.astype(BF16)
        lane = iota((SUB, LANES), 1)
        lane = jnp.where(lane < SUB, lane, lane - SUB)
        row = iota((SUB, LANES), 0)
        eye = jnp.where(row == lane, 1.0, 0.0)
        for k in range(tokens // SUB):
            rows = pl.ds(k * SUB, SUB)
            bk = b_ref[0, rows, :]
            sc = mm_nt(c_ref[0, rows, :], jnp.concatenate([bk, bk], axis=0))
            dk = doc[rows, :]
            drow = jnp.sum(dk * eye, axis=0, keepdims=True)
            gm[k] = jnp.where((row >= lane) & (dk == drow), sc, 0.0)
        low_lane = iota((SUB, LANES), 1) < SUB
        one_lane = iota((1, LANES), 1) < SUB

        def tile(t, _):
            skip = jnp.where(one_lane, gain_ref[2 * t], gain_ref[2 * t + 1])
            for s in range(spans):
                o = s * SPAN

                def level(at, width):
                    lo, hi = pl.ds(o + at, width), pl.ds(o + at + width, width)
                    run_lo, run_hi = cum[t, lo, :], cum[t, hi, :]
                    doc_lo, doc_hi = doc[lo, :], doc[hi, :]
                    ref, ref_doc = run_lo[width - 1 : width, :], doc_lo[width - 1 : width, :]
                    keep = jnp.where(doc_lo == ref_doc, jnp.exp2(ref - run_lo), 0.0)
                    enter = jnp.where(doc_hi == ref_doc, jnp.exp2(run_hi - ref), 0.0)
                    weighted = (xm[t, lo, :].astype(F32) * keep).astype(BF16)
                    part = gb[s, at + width : at + 2 * width, at : at + width]
                    return enter * mm(part, weighted)

                far = level(0, HALF)
                near = [level(0, SUB), level(HALF, SUB)]
                for q in range(SPAN // SUB):
                    rows = pl.ds(o + q * SUB, SUB)
                    run = cum[t, rows, :]
                    xq = xm[t, rows, :]
                    xf = xq.astype(F32)
                    run_row = jnp.sum(run * eye, axis=0, keepdims=True)
                    w = jnp.exp2(jnp.minimum(run - run_row, 0.0)) * gm[s * (SPAN // SUB) + q]
                    left = jnp.where(low_lane, xf, 0.0).astype(BF16)
                    right = jnp.where(low_lane, 0.0, xf).astype(BF16)
                    v = mm(w.astype(BF16), jnp.concatenate([left, right], axis=0))
                    v = v + skip * xf
                    if q % 2 == 1:
                        v = v + near[q // 2]
                    if q >= 2:
                        v = v + far[(q - 2) * SUB : (q - 1) * SUB, :]
                    y[t, rows, :] = v
            return 0

        lax.fori_loop(0, tiles, tile, 0)

    meet(0, 1)
    meet(2, 3)
    meet(4, 5)

    @pl.when(among(0, 2, 3, 4))
    def _():
        tout[0] = mown[...]
        send_t(0, to_lead, 0).start()

        def step(j, r):
            piece = rows_of(r)
            outb[0, j, piece, :] = comb[j, piece, :].astype(BF16)
            send(outb.at[0], 0, j, r, to_lead, 0).start()

        pieces(step)

    local_part()
    meet(1, 2, 3)
    meet(5, 6)
    meet(6, 7)

    @pl.when(among(1, 2, 3, 5, 6, 7))
    def _():
        send_t(0, to_lead, 0).wait_recv()

    def row(ref, j):
        return ref[0, pl.ds(j, 1), :]

    is_later = chip == 2

    @pl.when(among(1, 2, 5, 6))
    def _():
        got, own = parts_of(tin.at[0]), parts_of(mown)
        put(tout.at[1], join(pick(is_later, own, got), pick(is_later, got, own)))
        send_t(1, to_join, join_slot).start()

    def enter(j, r, e):
        piece = rows_of(r)
        f = row(mbase, j) * e + base[j, piece, :]
        eown[core * half + j, piece, :] = jnp.where(is_low, e, f).astype(BF16)
        psnd[j, piece, :] = jnp.where(is_low, f, e).astype(BF16)
        pass_copy(j, r).start()

    def join_step(j, r):
        piece = rows_of(r)
        send(outb.at[0], 0, j, r, to_lead, 0).wait_recv()
        got, own = inb[0, j, piece, :].astype(F32), comb[j, piece, :]
        scale = jnp.where(is_later, row(tin.at[0], j), row(mown, j))
        joined = scale * jnp.where(is_later, own, got) + jnp.where(is_later, got, own)
        outb[1, j, piece, :] = joined.astype(BF16)
        send(outb.at[1], 1, j, r, to_join, join_slot).start()

        @pl.when(chip == 1)
        def _():
            enter(j, r, got)

    @pl.when(among(2, 5, 6))
    def _():
        pieces(join_step)

    def pass_rows(side):
        return pltpu.make_async_remote_copy(
            src_ref=vsnd,
            dst_ref=vent.at[side],
            send_sem=wsem.at[0],
            recv_sem=wsem.at[1],
            device_id={"ctx": partner},
            device_id_type=MESH,
        )

    def enter_rows_of(e):
        for i in range(2):
            f = mbase[3] * e[i] + mbase[1 + i]
            vent[core, i] = jnp.where(is_low, e[i], f)
            vsnd[i] = jnp.where(is_low, f, e[i])
        pass_rows(core).start()

    @pl.when(chip == 0)
    def _():
        enter_rows_of((jnp.zeros((8, LANES), F32),) * 2)
        pieces(lambda j, r: enter(j, r, jnp.zeros((ROWS_STEP, LANES), F32)))

    def direct(j, r, to):
        @pl.when(j * steps + r >= half * steps - DIRECT)
        def _():
            send(outb.at[2], 3, j, r, to, 1).start()

    rest = []

    @pl.when(chip == 1)
    def _():
        enter_rows_of((tin[0, 1], tin[0, 2]))

        def last_step(j, r):
            piece = rows_of(r)
            send(outb.at[1], 1, j, r, 1, 1).wait_recv()
            got, own = inb[1, j, piece, :].astype(F32), outb[1, j, piece, :].astype(F32)
            outb[2, j, piece, :] = (row(tin.at[1], j) * own + got).astype(BF16)
            send(outb.at[2], 2, j, r, 7, 1).start()
            direct(j, r, 6)

        def both(j, r):
            join_step(j, r)
            last_step(j - behind // steps, r)

        behind = (half // 2) * steps
        pieces(join_step, 0, behind)
        send_t(1, 1, 1).wait_recv()
        meet(1, 6, 7)
        put(tout.at[2], join(parts_of(tout.at[1]), parts_of(tin.at[1])))
        send_t(2, 7, 1).start()
        pieces(both, behind, half * steps)
        pieces(lambda j, r: send(outb.at[1], 4, j, r, 2, 1).start(), half * steps - DIRECT, half * steps)
        rest.append(lambda: pieces(last_step, half * steps - behind, half * steps))

    joins = among(3, 5, 6, 7)

    def last_step(j, r):
        piece = rows_of(r)
        send(outb.at[2], 2, j, r, 1, 1).wait_recv()

        @pl.when(among(4, 7) & (j * steps + r < half * steps - DIRECT))
        def _():
            send(inb.at[1], 2, j, r, to_last, 1).start()

        @pl.when(among(3, 7))
        def _():
            send(outb.at[0], 0, j, r, to_lead, 0).wait_recv()

        got = inb[1, j, piece, :].astype(F32)
        add = jnp.where(joins, inb[0, j, piece, :].astype(F32), 0.0)
        e = jnp.where(joins, row(tin.at[0], j), 1.0) * got + add

        @pl.when(chip == 3)
        def _():
            outb[2, j, piece, :] = (row(mown, j) * e + comb[j, piece, :]).astype(BF16)
            send(outb.at[2], 2, j, r, 4, 1).start()
            direct(j, r, 5)

            @pl.when(j * steps + r < half * steps - DIRECT)
            def _():
                send(inb.at[1], 4, j, r, 2, 1).start()

        enter(j, r, e)

    @pl.when(chip >= 2)
    def _():
        send_t(2, 1, 1).wait_recv()
        meet(3, 4, 5)

        @pl.when(among(4, 7))
        def _():
            tout[2] = tin[1]
            send_t(2, to_last, 1).start()

        e = parts_of(tin.at[1])
        e = pick(joins, join(e, parts_of(tin.at[0])), e)

        @pl.when(chip == 3)
        def _():
            put(tout.at[2], join(e, parts_of(mown)))
            send_t(2, to_last, 1).start()
            back_t().start()

        enter_rows_of(e[1:3])
        pieces(last_step, 0, SCORES_AT)

    pass_rows(1 - core).wait_recv()
    entering = jnp.concatenate(
        [jnp.concatenate([vent[h, 0], vent[h, 1]], axis=1) for h in range(2)], axis=0
    )
    local_rows = jnp.zeros((head_rows, tokens), F32)
    for t in range(tiles):
        weight = jnp.broadcast_to(rd[t : t + 1, :], (head_rows, LANES)).astype(BF16)
        local_rows = local_rows + mm_nt(weight, y[t].astype(BF16))
    row_scores = []
    for s in range(spans):
        if s > 0:
            entering = enter_rows[0][:, SPAN - 1 : SPAN] * entering + read_states[0]
        far = mm_nt(entering.astype(BF16), c_ref[0, pl.ds(s * SPAN, SPAN), :]) * enter_rows[s]
        far = jnp.sum(far, axis=0, keepdims=True)
        row_scores.append(far + local_rows[0:1, s * SPAN : (s + 1) * SPAN])
    row_scores = jnp.where(live_row, jnp.concatenate(row_scores, axis=1), 0.0)
    for i in range(tokens // LANES):
        sums[mine, i : i + 1, :] = row_scores[:, i * LANES : (i + 1) * LANES]

    def score_copy(k):
        return pltpu.make_async_remote_copy(
            src_ref=sums.at[mine],
            dst_ref=sums.at[mine],
            send_sem=ysem_s.at[k],
            recv_sem=ysem_r.at[k],
            device_id={"head": lax.rem(mine + k, heads_axis)},
            device_id_type=MESH,
        )

    @pl.when(rank(mine) < heads_axis - 1)
    def _():
        pl.semaphore_wait(yready, heads_axis - 1 - rank(mine))

    for k in range(1, heads_axis):
        score_copy(k).start()

    @pl.when(chip == 1)
    def _():
        for run in rest:
            run()

    @pl.when(chip >= 2)
    def _():
        pieces(last_step, SCORES_AT, half * steps)

    def out_copy(t):
        return pltpu.make_async_copy(
            out_ref.at[t],
            out_hbm.at[0, :, pl.ds(pl.multiple_of(t * LANES, LANES), LANES)],
            osem.at[t],
        )

    def finish_tile(t):
        cols = pl.ds(pl.multiple_of(t * LANES, LANES), LANES)
        e0 = eown[t]
        e1 = (ta[t][0:1, :] * e0.astype(F32) + first[t]).astype(BF16)
        for s, e in enumerate((e0, e1)):
            rows = pl.ds(s * SPAN, SPAN)
            enter = jnp.where(doc[rows, :] == 0.0, jnp.exp2(cum[t, rows, :]), 0.0)
            v = y[t, rows, :] + enter * mm(c_ref[0, rows, :], e)
            v = jnp.where(live[s * SPAN : (s + 1) * SPAN, :], v, 0.0).astype(BF16)
            out_ref[t, rows, :] = v
        out_copy(t).start()

    for j in range(half):
        finish_tile(core * half + j)
    for j in range(half):
        for r in range(steps):
            piece = pl.ds(r * ROWS_STEP, ROWS_STEP)
            pltpu.make_async_remote_copy(
                src_ref=psnd.at[j, piece],
                dst_ref=eown.at[(1 - core) * half + j, piece],
                send_sem=fsem_s.at[j, r],
                recv_sem=fsem_r.at[j, r],
                device_id={"ctx": partner},
                device_id_type=MESH,
            ).wait_recv()
        finish_tile((1 - core) * half + j)

    for k in range(1, heads_axis):
        score_copy(k).wait()
    total = sums[0]
    for k in range(1, heads_axis):
        total = total + sums[k]
    for i in range(tokens // LANES):
        score_ref[:, i * LANES : (i + 1) * LANES] = total[i : i + 1, :]

    for t in range(tiles):
        out_copy(t).wait()
    for j in range(half):
        state_copy(sbf, srecv, psem_s, psem_r, j, partner).wait_send()
    t_copy.wait_send()
    pieces(lambda j, r: pass_copy(j, r).wait_send())

    @pl.when(among(0, 2, 3, 4))
    def _():
        send_t(0, to_lead, 0).wait_send()
        pieces(lambda j, r: send(outb.at[0], 0, j, r, to_lead, 0).wait_send())

    pass_rows(core).wait_send()

    @pl.when(among(1, 2, 5, 6))
    def _():
        send_t(1, to_join, join_slot).wait_send()
        pieces(lambda j, r: send(outb.at[1], 1, j, r, to_join, join_slot).wait_send())

    @pl.when(among(1, 3, 4, 7))
    def _():
        send_t(2, to_last, 1).wait_send()
        pieces(lambda j, r: send(outb.at[2], 2, j, r, to_last, 1).wait_send(), 0, half * steps - DIRECT)

    @pl.when(among(1, 3))
    def _():
        for out in (2, 3):
            pieces(
                lambda j, r: send(outb.at[2], out, j, r, 5, 1).wait_send(),
                half * steps - DIRECT,
                half * steps,
            )

    @pl.when(chip == 3)
    def _():
        back_t().wait_send()
        pieces(lambda j, r: send(inb.at[1], 4, j, r, 2, 1).wait_send(), 0, half * steps - DIRECT)

    @pl.when(chip == 1)
    def _():
        pieces(
            lambda j, r: send(outb.at[1], 4, j, r, 2, 1).wait_send(),
            half * steps - DIRECT,
            half * steps,
        )


def state_copy(src, dst, send, recv, j, partner):
    return pltpu.make_async_remote_copy(
        src_ref=src.at[j],
        dst_ref=dst.at[j],
        send_sem=send.at[j],
        recv_sem=recv.at[j],
        device_id={"ctx": partner},
        device_id_type=MESH,
    )


def body(inputs, b_proj, c_proj, log_decay, starts, counts, skip_gain, readout):
    tokens, width = inputs.shape[1:]
    ctxs, heads_axis = lax.axis_size("ctx"), lax.axis_size("head")
    tiles = width // LANES
    half = tiles // 2
    spans = tokens // SPAN
    steps = SPAN // ROWS_STEP
    vmem, smem = pl.BlockSpec(memory_space=pltpu.VMEM), pl.BlockSpec(memory_space=pltpu.SMEM)
    hbm = pl.BlockSpec(memory_space=pltpu.HBM)
    big = lambda n, dtype: pltpu.VMEM((n, SPAN, LANES), dtype)
    small = lambda n: pltpu.VMEM((n, 8, LANES), F32)
    sem = pltpu.SemaphoreType.DMA
    return pl.pallas_call(
        functools.partial(kernel, (ctxs, heads_axis, tokens, tiles)),
        out_shape=(
            jax.ShapeDtypeStruct(inputs.shape, BF16),
            jax.ShapeDtypeStruct((1, tokens), F32),
        ),
        in_specs=[smem, hbm, hbm, hbm, hbm, hbm, smem, hbm],
        out_specs=(pl.BlockSpec(memory_space=pltpu.HBM), vmem),
        scratch_shapes=[
            pltpu.VMEM((tiles, tokens, LANES), BF16),
            sem((tiles,)),
            pltpu.VMEM(inputs.shape, BF16),
            pltpu.VMEM(b_proj.shape, BF16),
            pltpu.VMEM(c_proj.shape, BF16),
            pltpu.VMEM(log_decay.shape, BF16),
            pltpu.VMEM(starts.shape, starts.dtype),
            pltpu.VMEM((tiles, LANES), BF16),
            sem((6,)),
            pltpu.VMEM((tiles, tokens, LANES), BF16),
            pltpu.VMEM((tokens, width), BF16),
            pltpu.VMEM((tiles, tokens, LANES), F32),
            pltpu.VMEM((tokens, LANES), F32),
            pltpu.VMEM((SPAN, tokens), BF16),
            big(tiles, F32),
            big(tiles, F32),
            small(tiles),
            small(tiles),
            big(half, BF16),
            big(half, BF16),
            pltpu.VMEM((2, 4, 8, LANES), F32),
            small(4),
            small(4),
            big(half, F32),
            big(half, F32),
            small(4),
            small(4),
            pltpu.VMEM((2, half, SPAN, LANES), BF16),
            pltpu.VMEM((2, 4, 8, LANES), F32),
            pltpu.VMEM((3, half, SPAN, LANES), BF16),
            pltpu.VMEM((3, 4, 8, LANES), F32),
            big(tiles, BF16),
            big(half, BF16),
            pltpu.VMEM((2, 2, 8, LANES), F32),
            small(2),
            pltpu.VMEM((tiles, tokens, LANES), F32),
            pltpu.VMEM((spans, SPAN, SPAN), BF16),
            pltpu.VMEM((tokens // SUB, SUB, LANES), F32),
            pltpu.VMEM((heads_axis, tokens // LANES, LANES), F32),
            pltpu.VMEM((tiles, LANES), F32),
            sem((half,)), sem((half,)), sem((2,)),
            sem((5, half, steps)), sem((2, half, steps)), sem((4,)), sem((2,)),
            sem((half, steps)), sem((half, steps)), sem((2,)),
            pltpu.SemaphoreType.REGULAR((ctxs // 2,)), pltpu.SemaphoreType.REGULAR,
            sem((heads_axis,)), sem((heads_axis,)),
        ],
        compiler_params=pltpu.CompilerParams(collective_id=0, has_side_effects=True),
        name="ssd",
    )(counts, inputs, b_proj, c_proj, log_decay, starts, skip_gain, readout.reshape(tiles, LANES))


def solution(mesh):
    placed = (
        P("rep", "ctx", "head"),
        P("rep", "ctx", "head"),
        P("rep", "ctx", "head"),
        P("rep", "head", "ctx"),
        P("rep", "ctx"),
        P("rep", "ctx"),
        P("head"),
        P("head"),
    )
    return jax.shard_map(
        body,
        mesh=mesh,
        in_specs=placed,
        out_specs=(P("rep", "ctx", "head"), P("rep", "ctx")),
        check_vma=False,
    )
```

```python
import functools
import math

import jax
import jax.numpy as jnp
from jax import lax
from jax.experimental import pallas as pl
from jax.experimental.pallas import tpu as pltpu
from jax.sharding import PartitionSpec as P

SPAN = 256
HALF = 128
SUB = 64
LANES = 128
ROWS_STEP = 64
SCORES_AT = 3
DIRECT = 6
EDGES = ((0, 1), (1, 2), (2, 3), (1, 3), (1, 6), (1, 7), (3, 4), (3, 5), (4, 5), (5, 6), (6, 7))
LOG2E = math.log2(math.e)
F32 = jnp.float32
BF16 = jnp.bfloat16
MESH = pl.DeviceIdType.MESH


def mm(a, b):
    return lax.dot_general(a, b, (((1,), (0,)), ((), ())), preferred_element_type=F32)


def mm_nt(a, b):
    return lax.dot_general(a, b, (((1,), (1,)), ((), ())), preferred_element_type=F32)


def mm_tn(a, b):
    return lax.dot_general(a, b, (((0,), (0,)), ((), ())), preferred_element_type=F32)


def iota(shape, dim):
    return lax.broadcasted_iota(jnp.int32, shape, dim)


def kernel(
    sizes,
    count_ref, x_hbm, b_hbm, c_hbm, a_hbm, s_hbm, gain_ref, read_hbm,
    out_hbm, score_ref,
    out_ref, osem,
    x_ref, b_ref, c_ref, a_ref, s_ref, read_ref, isem,
    xm, lx, cum, doc, bt, first, whole, ta, td, sbf, srecv, mfull, msnd, mrecv,
    comb, base, mown, mbase, inb, tin, outb, tout, eown, psnd, vent, vsnd, y, gb, gm, sums, rd,
    psem_s, psem_r, tsem, csem_s, csem_r, vsem_s, vsem_r, fsem_s, fsem_r, wsem, ready, yready, ysem_s, ysem_r,
):
    ctxs, heads_axis, tokens, tiles = sizes
    half = tiles // 2
    spans = tokens // SPAN
    steps = SPAN // ROWS_STEP
    ctx = lax.axis_index("ctx")
    core = lax.rem(ctx, 2)
    chip = ctx // 2
    mine = lax.axis_index("head")
    partner = ctx + 1 - 2 * core

    loads = [
        pltpu.make_async_copy(source, target, isem.at[i])
        for i, (source, target) in enumerate(
            ((a_hbm, a_ref), (s_hbm, s_ref), (read_hbm, read_ref), (b_hbm, b_ref), (x_hbm, x_ref), (c_hbm, c_ref))
        )
    ]
    for load in loads:
        load.start()
    barrier = pltpu.get_barrier_semaphore()
    middle = heads_axis // 2

    def rank(i):
        return jnp.where(i < middle, i, heads_axis + middle - 1 - i)

    others = [lax.rem(mine + k, heads_axis) for k in range(heads_axis)]
    pl.semaphore_signal(barrier, inc=1, device_id={"ctx": partner}, device_id_type=MESH)
    peers = 1 + rank(mine)
    for here, there in EDGES:
        peers = peers + jnp.where(chip == there, 1, 0)

        @pl.when(chip == here)
        def _():
            pl.semaphore_signal(
                barrier, inc=1, device_id={"ctx": 2 * there + core}, device_id_type=MESH
            )

    for other in others[1:]:
        @pl.when(rank(other) > rank(mine))
        def _():
            pl.semaphore_signal(barrier, inc=1, device_id={"head": other}, device_id_type=MESH)

    count = count_ref[0, 0]
    live_row = iota((1, tokens), 1) < count
    loads[0].wait()
    loads[1].wait()
    log_decay = jnp.where(live_row, a_ref[0].astype(F32), 0.0).astype(BF16)
    starts = jnp.where(live_row, s_ref[...].astype(F32), 0.0)
    head_rows = log_decay.shape[0]
    all_starts = jnp.broadcast_to(starts, (head_rows, tokens)).astype(BF16)
    starts = jnp.where(iota((head_rows, tokens), 0) == 0, starts, 0.0).astype(BF16)
    spread = (iota((head_rows, tiles * LANES), 0) == iota((head_rows, tiles * LANES), 1) // SUB)
    spread = jnp.where(spread, 1.0, 0.0).astype(BF16)
    ones = jnp.ones((head_rows, LANES), BF16)
    tri = jnp.where(iota((SPAN, SPAN), 0) >= iota((SPAN, SPAN), 1), 1.0, 0.0).astype(BF16)
    for s in range(spans):
        rows = pl.ds(s * SPAN, SPAN)
        lx[rows, :] = mm_tn(log_decay[:, s * SPAN : (s + 1) * SPAN], spread).astype(BF16)
        spread_starts = mm_tn(starts[:, s * SPAN : (s + 1) * SPAN], ones).astype(BF16)
        doc[rows, :] = mm(tri, spread_starts)
    loads[3].wait()
    for s in range(spans):
        rows = pl.ds(s * SPAN, SPAN)
        bt[:, rows] = b_ref[0, rows, :].astype(F32).T.astype(BF16)
    loads[2].wait()
    loads[4].wait()

    live = iota((tokens, LANES), 0) < count

    pl.semaphore_wait(barrier, peers)
    for here, there in EDGES:
        @pl.when(chip == there)
        def _():
            pl.semaphore_signal(
                ready.at[there], inc=1, device_id={"ctx": 2 * here + core}, device_id_type=MESH
            )

    for other in others[1:]:
        @pl.when(rank(other) < rank(mine))
        def _():
            pl.semaphore_signal(yready, inc=1, device_id={"head": other}, device_id_type=MESH)

    def meet(here, *there):
        @pl.when(chip == here)
        def _():
            for other in there:
                pl.semaphore_wait(ready.at[other], 1)

    def state_tile(t):
        cols = pl.ds(pl.multiple_of(t * LANES, LANES), LANES)
        xt = jnp.where(live, x_ref[0, :, cols].astype(F32), 0.0).astype(BF16)
        xm[t] = xt
        states, totals = [], []
        for s in range(spans):
            rows = slice(s * SPAN, (s + 1) * SPAN)
            run = mm(tri, lx[pl.ds(s * SPAN, SPAN), cols]) * LOG2E
            cum[t, pl.ds(s * SPAN, SPAN), :] = run
            docs = doc[pl.ds(s * SPAN, SPAN), :]
            last = run[SPAN - 1 : SPAN, :]
            keep = jnp.where(docs == docs[SPAN - 1 : SPAN, :], jnp.exp2(last - run), 0.0)
            weighted = (xt[rows, :].astype(F32) * keep).astype(BF16)
            states.append(mm(bt[:, pl.ds(s * SPAN, SPAN)], weighted))
            totals.append(jnp.where(docs[SPAN - 1 : SPAN, :] == 0.0, jnp.exp2(last), 0.0))
        first[t] = states[0]
        joined = totals[1] * states[0] + states[1]
        whole[t] = joined
        ta[t] = jnp.broadcast_to(totals[0], (8, LANES))
        td[t] = jnp.broadcast_to(totals[0] * totals[1], (8, LANES))
        return joined

    for j in range(half):
        sbf[j] = state_tile((1 - core) * half + j).astype(BF16)
        state_copy(sbf, srecv, psem_s, psem_r, j, partner).start()
    rd[...] = read_ref[...].astype(F32)
    upper = jnp.where(iota((SPAN, SPAN), 0) <= iota((SPAN, SPAN), 1), 1.0, 0.0).astype(BF16)
    head_of = iota((head_rows, LANES), 1) // SUB
    read_rows = jnp.zeros((head_rows, tokens), F32)
    for t in range(tiles):
        part = jnp.where(iota((head_rows, LANES), 0) == 2 * t + head_of, rd[t : t + 1, :], 0.0)
        read_rows = read_rows + mm_nt(part.astype(BF16), x_ref[0, :, t * LANES : (t + 1) * LANES])
    read_rows = jnp.where(live_row, read_rows, 0.0)
    enter_rows, read_states, row_totals = [], [], []
    for s in range(spans):
        lanes = slice(s * SPAN, (s + 1) * SPAN)
        run = mm(log_decay[:, lanes], upper) * LOG2E
        docs = mm(all_starts[:, lanes], upper)
        enter_rows.append(jnp.where(docs == 0.0, jnp.exp2(run), 0.0))
        ends = slice(SPAN - 1, SPAN)
        keep = jnp.where(docs == docs[:, ends], jnp.exp2(run[:, ends] - run), 0.0)
        read_states.append(mm((read_rows[:, lanes] * keep).astype(BF16), b_ref[0, pl.ds(s * SPAN, SPAN), :]))
        row_totals.append(jnp.broadcast_to(enter_rows[s][:, ends], (head_rows, LANES)))
    read_state = enter_rows[1][:, SPAN - 1 : SPAN] * read_states[0] + read_states[1]
    for h in range(2):
        rows = slice(h * 8, (h + 1) * 8)
        for i in range(2):
            mfull[h, 1 + i] = read_state[rows, i * LANES : (i + 1) * LANES]
        mfull[h, 3] = row_totals[0][rows] * row_totals[1][rows]

    t_copy = pltpu.make_async_remote_copy(
        src_ref=msnd,
        dst_ref=mrecv,
        send_sem=tsem.at[0],
        recv_sem=tsem.at[1],
        device_id={"ctx": partner},
        device_id_type=MESH,
    )
    msnd[...] = mfull[1 - core]
    for j in range(half):
        msnd[0, j : j + 1, :] = td[(1 - core) * half + j][0:1, :]
    t_copy.start()
    for j in range(half):
        state_tile(core * half + j)
        mfull[core, 0, j : j + 1, :] = td[core * half + j][0:1, :]

    def join(earlier, later):
        columns = later[3]
        return (
            later[0] * earlier[0],
            columns * earlier[1] + later[1],
            columns * earlier[2] + later[2],
            columns * earlier[3],
        )

    def put(ref, parts):
        for i, part in enumerate(parts):
            ref[i] = part

    def pick(choose, a, b):
        return tuple(jnp.where(choose, u, v) for u, v in zip(a, b))

    def parts_of(ref):
        return tuple(ref[i] for i in range(4))

    t_copy.wait_recv()
    is_low = core == 0
    own_parts, their_parts = parts_of(mfull.at[core]), parts_of(mrecv)
    low_parts, high_parts = pick(is_low, own_parts, their_parts), pick(is_low, their_parts, own_parts)
    put(mown, join(low_parts, high_parts))
    put(mbase, low_parts)
    for j in range(half):
        state_copy(sbf, srecv, psem_s, psem_r, j, partner).wait_recv()
        own, theirs = whole[core * half + j], srecv[j].astype(F32)
        low, high = jnp.where(is_low, own, theirs), jnp.where(is_low, theirs, own)
        comb[j] = high_parts[0][j : j + 1, :] * low + high
        base[j] = low

    def send(src, out, j, r, to, slot):
        piece = rows_of(r)
        return pltpu.make_async_remote_copy(
            src_ref=src.at[j, piece],
            dst_ref=inb.at[slot, j, piece],
            send_sem=csem_s.at[out, j, r],
            recv_sem=csem_r.at[slot, j, r],
            device_id={"ctx": 2 * to + core},
            device_id_type=MESH,
        )

    def send_t(out, to, slot):
        return pltpu.make_async_remote_copy(
            src_ref=tout.at[out],
            dst_ref=tin.at[slot],
            send_sem=vsem_s.at[out],
            recv_sem=vsem_r.at[slot],
            device_id={"ctx": 2 * to + core},
            device_id_type=MESH,
        )

    def back_t():
        return pltpu.make_async_remote_copy(
            src_ref=tin.at[1],
            dst_ref=tin.at[1],
            send_sem=vsem_s.at[3],
            recv_sem=vsem_r.at[1],
            device_id={"ctx": 4 + core},
            device_id_type=MESH,
        )

    def pieces(step, begin=0, end=half * steps):
        def one(q, _):
            step(q // steps, lax.rem(q, steps))
            return 0

        lax.fori_loop(begin, end, one, 0)

    def rows_of(r):
        return pl.ds(pl.multiple_of(r * ROWS_STEP, ROWS_STEP), ROWS_STEP)

    def of_chip(*values):
        result = values[-1]
        for i, value in enumerate(values[:-1]):
            result = jnp.where(chip == i, value, result)
        return result

    def among(*chips):
        return functools.reduce(jnp.logical_or, [chip == i for i in chips])

    to_lead = of_chip(1, 0, 3, 2, 5, 4, 4, 4)
    to_join = of_chip(1, 3, 1, 1, 4, 6, 7, 6)
    join_slot = jnp.where(chip < 3, 1, 0)
    to_last = of_chip(1, 7, 1, 4, 5, 4, 4, 6)

    def pass_copy(j, r):
        piece = rows_of(r)
        return pltpu.make_async_remote_copy(
            src_ref=psnd.at[j, piece],
            dst_ref=eown.at[core * half + j, piece],
            send_sem=fsem_s.at[j, r],
            recv_sem=fsem_r.at[j, r],
            device_id={"ctx": partner},
            device_id_type=MESH,
        )

    def local_part():
        loads[5].wait()
        for s in range(spans):
            rows = pl.ds(s * SPAN, SPAN)
            scores = mm_nt(c_ref[0, rows, :], b_ref[0, rows, :])
            gb[s] = scores.astype(BF16)
        lane = iota((SUB, LANES), 1)
        lane = jnp.where(lane < SUB, lane, lane - SUB)
        row = iota((SUB, LANES), 0)
        eye = jnp.where(row == lane, 1.0, 0.0)
        for k in range(tokens // SUB):
            rows = pl.ds(k * SUB, SUB)
            bk = b_ref[0, rows, :]
            sc = mm_nt(c_ref[0, rows, :], jnp.concatenate([bk, bk], axis=0))
            dk = doc[rows, :]
            drow = jnp.sum(dk * eye, axis=0, keepdims=True)
            gm[k] = jnp.where((row >= lane) & (dk == drow), sc, 0.0)
        low_lane = iota((SUB, LANES), 1) < SUB
        one_lane = iota((1, LANES), 1) < SUB

        def tile(t, _):
            skip = jnp.where(one_lane, gain_ref[2 * t], gain_ref[2 * t + 1])
            for s in range(spans):
                o = s * SPAN

                def level(at, width):
                    lo, hi = pl.ds(o + at, width), pl.ds(o + at + width, width)
                    run_lo, run_hi = cum[t, lo, :], cum[t, hi, :]
                    doc_lo, doc_hi = doc[lo, :], doc[hi, :]
                    ref, ref_doc = run_lo[width - 1 : width, :], doc_lo[width - 1 : width, :]
                    keep = jnp.where(doc_lo == ref_doc, jnp.exp2(ref - run_lo), 0.0)
                    enter = jnp.where(doc_hi == ref_doc, jnp.exp2(run_hi - ref), 0.0)
                    weighted = (xm[t, lo, :].astype(F32) * keep).astype(BF16)
                    part = gb[s, at + width : at + 2 * width, at : at + width]
                    return enter * mm(part, weighted)

                far = level(0, HALF)
                near = [level(0, SUB), level(HALF, SUB)]
                for q in range(SPAN // SUB):
                    rows = pl.ds(o + q * SUB, SUB)
                    run = cum[t, rows, :]
                    xq = xm[t, rows, :]
                    xf = xq.astype(F32)
                    run_row = jnp.sum(run * eye, axis=0, keepdims=True)
                    w = jnp.exp2(jnp.minimum(run - run_row, 0.0)) * gm[s * (SPAN // SUB) + q]
                    left = jnp.where(low_lane, xf, 0.0).astype(BF16)
                    right = jnp.where(low_lane, 0.0, xf).astype(BF16)
                    v = mm(w.astype(BF16), jnp.concatenate([left, right], axis=0))
                    v = v + skip * xf
                    if q % 2 == 1:
                        v = v + near[q // 2]
                    if q >= 2:
                        v = v + far[(q - 2) * SUB : (q - 1) * SUB, :]
                    y[t, rows, :] = v
            return 0

        lax.fori_loop(0, tiles, tile, 0)

    meet(0, 1)
    meet(2, 3)
    meet(4, 5)

    @pl.when(among(0, 2, 3, 4))
    def _():
        tout[0] = mown[...]
        send_t(0, to_lead, 0).start()

        def step(j, r):
            piece = rows_of(r)
            outb[0, j, piece, :] = comb[j, piece, :].astype(BF16)
            send(outb.at[0], 0, j, r, to_lead, 0).start()

        pieces(step)

    local_part()
    meet(1, 2, 3)
    meet(5, 6)
    meet(6, 7)

    @pl.when(among(1, 2, 3, 5, 6, 7))
    def _():
        send_t(0, to_lead, 0).wait_recv()

    def row(ref, j):
        return ref[0, pl.ds(j, 1), :]

    is_later = chip == 2

    @pl.when(among(1, 2, 5, 6))
    def _():
        got, own = parts_of(tin.at[0]), parts_of(mown)
        put(tout.at[1], join(pick(is_later, own, got), pick(is_later, got, own)))
        send_t(1, to_join, join_slot).start()

    def enter(j, r, e):
        piece = rows_of(r)
        f = row(mbase, j) * e + base[j, piece, :]
        eown[core * half + j, piece, :] = jnp.where(is_low, e, f).astype(BF16)
        psnd[j, piece, :] = jnp.where(is_low, f, e).astype(BF16)
        pass_copy(j, r).start()

    def join_step(j, r):
        piece = rows_of(r)
        send(outb.at[0], 0, j, r, to_lead, 0).wait_recv()
        got, own = inb[0, j, piece, :].astype(F32), comb[j, piece, :]
        scale = jnp.where(is_later, row(tin.at[0], j), row(mown, j))
        joined = scale * jnp.where(is_later, own, got) + jnp.where(is_later, got, own)
        outb[1, j, piece, :] = joined.astype(BF16)
        send(outb.at[1], 1, j, r, to_join, join_slot).start()

        @pl.when(chip == 1)
        def _():
            enter(j, r, got)

    @pl.when(among(2, 5, 6))
    def _():
        pieces(join_step)

    def pass_rows(side):
        return pltpu.make_async_remote_copy(
            src_ref=vsnd,
            dst_ref=vent.at[side],
            send_sem=wsem.at[0],
            recv_sem=wsem.at[1],
            device_id={"ctx": partner},
            device_id_type=MESH,
        )

    def enter_rows_of(e):
        for i in range(2):
            f = mbase[3] * e[i] + mbase[1 + i]
            vent[core, i] = jnp.where(is_low, e[i], f)
            vsnd[i] = jnp.where(is_low, f, e[i])
        pass_rows(core).start()

    @pl.when(chip == 0)
    def _():
        enter_rows_of((jnp.zeros((8, LANES), F32),) * 2)
        pieces(lambda j, r: enter(j, r, jnp.zeros((ROWS_STEP, LANES), F32)))

    def direct(j, r, to):
        @pl.when(j * steps + r >= half * steps - DIRECT)
        def _():
            send(outb.at[2], 3, j, r, to, 1).start()

    rest = []

    @pl.when(chip == 1)
    def _():
        enter_rows_of((tin[0, 1], tin[0, 2]))

        def last_step(j, r):
            piece = rows_of(r)
            send(outb.at[1], 1, j, r, 1, 1).wait_recv()
            got, own = inb[1, j, piece, :].astype(F32), outb[1, j, piece, :].astype(F32)
            outb[2, j, piece, :] = (row(tin.at[1], j) * own + got).astype(BF16)
            send(outb.at[2], 2, j, r, 7, 1).start()
            direct(j, r, 6)

        def both(j, r):
            join_step(j, r)
            last_step(j - behind // steps, r)

        behind = (half // 2) * steps
        pieces(join_step, 0, behind)
        send_t(1, 1, 1).wait_recv()
        meet(1, 6, 7)
        put(tout.at[2], join(parts_of(tout.at[1]), parts_of(tin.at[1])))
        send_t(2, 7, 1).start()
        pieces(both, behind, half * steps)
        pieces(lambda j, r: send(outb.at[1], 4, j, r, 2, 1).start(), half * steps - DIRECT, half * steps)
        rest.append(lambda: pieces(last_step, half * steps - behind, half * steps))

    joins = among(3, 5, 6, 7)

    def last_step(j, r):
        piece = rows_of(r)
        send(outb.at[2], 2, j, r, 1, 1).wait_recv()

        @pl.when(among(4, 7) & (j * steps + r < half * steps - DIRECT))
        def _():
            send(inb.at[1], 2, j, r, to_last, 1).start()

        @pl.when(among(3, 7))
        def _():
            send(outb.at[0], 0, j, r, to_lead, 0).wait_recv()

        got = inb[1, j, piece, :].astype(F32)
        add = jnp.where(joins, inb[0, j, piece, :].astype(F32), 0.0)
        e = jnp.where(joins, row(tin.at[0], j), 1.0) * got + add

        @pl.when(chip == 3)
        def _():
            outb[2, j, piece, :] = (row(mown, j) * e + comb[j, piece, :]).astype(BF16)
            send(outb.at[2], 2, j, r, 4, 1).start()
            direct(j, r, 5)

            @pl.when(j * steps + r < half * steps - DIRECT)
            def _():
                send(inb.at[1], 4, j, r, 2, 1).start()

        enter(j, r, e)

    @pl.when(chip >= 2)
    def _():
        send_t(2, 1, 1).wait_recv()
        meet(3, 4, 5)

        @pl.when(among(4, 7))
        def _():
            tout[2] = tin[1]
            send_t(2, to_last, 1).start()

        e = parts_of(tin.at[1])
        e = pick(joins, join(e, parts_of(tin.at[0])), e)

        @pl.when(chip == 3)
        def _():
            put(tout.at[2], join(e, parts_of(mown)))
            send_t(2, to_last, 1).start()
            back_t().start()

        enter_rows_of(e[1:3])
        pieces(last_step, 0, SCORES_AT)

    pass_rows(1 - core).wait_recv()
    entering = jnp.concatenate(
        [jnp.concatenate([vent[h, 0], vent[h, 1]], axis=1) for h in range(2)], axis=0
    )
    local_rows = jnp.zeros((head_rows, tokens), F32)
    for t in range(tiles):
        weight = jnp.broadcast_to(rd[t : t + 1, :], (head_rows, LANES)).astype(BF16)
        local_rows = local_rows + mm_nt(weight, y[t].astype(BF16))
    row_scores = []
    for s in range(spans):
        if s > 0:
            entering = enter_rows[0][:, SPAN - 1 : SPAN] * entering + read_states[0]
        far = mm_nt(entering.astype(BF16), c_ref[0, pl.ds(s * SPAN, SPAN), :]) * enter_rows[s]
        far = jnp.sum(far, axis=0, keepdims=True)
        row_scores.append(far + local_rows[0:1, s * SPAN : (s + 1) * SPAN])
    row_scores = jnp.where(live_row, jnp.concatenate(row_scores, axis=1), 0.0)
    for i in range(tokens // LANES):
        sums[mine, i : i + 1, :] = row_scores[:, i * LANES : (i + 1) * LANES]

    def score_copy(k):
        return pltpu.make_async_remote_copy(
            src_ref=sums.at[mine],
            dst_ref=sums.at[mine],
            send_sem=ysem_s.at[k],
            recv_sem=ysem_r.at[k],
            device_id={"head": lax.rem(mine + k, heads_axis)},
            device_id_type=MESH,
        )

    @pl.when(rank(mine) < heads_axis - 1)
    def _():
        pl.semaphore_wait(yready, heads_axis - 1 - rank(mine))

    for k in range(1, heads_axis):
        score_copy(k).start()

    @pl.when(chip == 1)
    def _():
        for run in rest:
            run()

    @pl.when(chip >= 2)
    def _():
        pieces(last_step, SCORES_AT, half * steps)

    def out_copy(t):
        return pltpu.make_async_copy(
            out_ref.at[t],
            out_hbm.at[0, :, pl.ds(pl.multiple_of(t * LANES, LANES), LANES)],
            osem.at[t],
        )

    def finish_tile(t):
        cols = pl.ds(pl.multiple_of(t * LANES, LANES), LANES)
        e0 = eown[t]
        e1 = (ta[t][0:1, :] * e0.astype(F32) + first[t]).astype(BF16)
        for s, e in enumerate((e0, e1)):
            rows = pl.ds(s * SPAN, SPAN)
            enter = jnp.where(doc[rows, :] == 0.0, jnp.exp2(cum[t, rows, :]), 0.0)
            v = y[t, rows, :] + enter * mm(c_ref[0, rows, :], e)
            v = jnp.where(live[s * SPAN : (s + 1) * SPAN, :], v, 0.0).astype(BF16)
            out_ref[t, rows, :] = v
        out_copy(t).start()

    for j in range(half):
        finish_tile(core * half + j)
    for j in range(half):
        for r in range(steps):
            piece = pl.ds(r * ROWS_STEP, ROWS_STEP)
            pltpu.make_async_remote_copy(
                src_ref=psnd.at[j, piece],
                dst_ref=eown.at[(1 - core) * half + j, piece],
                send_sem=fsem_s.at[j, r],
                recv_sem=fsem_r.at[j, r],
                device_id={"ctx": partner},
                device_id_type=MESH,
            ).wait_recv()
        finish_tile((1 - core) * half + j)

    for k in range(1, heads_axis):
        score_copy(k).wait()
    total = sums[0]
    for k in range(1, heads_axis):
        total = total + sums[k]
    for i in range(tokens // LANES):
        score_ref[:, i * LANES : (i + 1) * LANES] = total[i : i + 1, :]

    for t in range(tiles):
        out_copy(t).wait()
    for j in range(half):
        state_copy(sbf, srecv, psem_s, psem_r, j, partner).wait_send()
    t_copy.wait_send()
    pieces(lambda j, r: pass_copy(j, r).wait_send())

    @pl.when(among(0, 2, 3, 4))
    def _():
        send_t(0, to_lead, 0).wait_send()
        pieces(lambda j, r: send(outb.at[0], 0, j, r, to_lead, 0).wait_send())

    pass_rows(core).wait_send()

    @pl.when(among(1, 2, 5, 6))
    def _():
        send_t(1, to_join, join_slot).wait_send()
        pieces(lambda j, r: send(outb.at[1], 1, j, r, to_join, join_slot).wait_send())

    @pl.when(among(1, 3, 4, 7))
    def _():
        send_t(2, to_last, 1).wait_send()
        pieces(lambda j, r: send(outb.at[2], 2, j, r, to_last, 1).wait_send(), 0, half * steps - DIRECT)

    @pl.when(among(1, 3))
    def _():
        for out in (2, 3):
            pieces(
                lambda j, r: send(outb.at[2], out, j, r, 5, 1).wait_send(),
                half * steps - DIRECT,
                half * steps,
            )

    @pl.when(chip == 3)
    def _():
        back_t().wait_send()
        pieces(lambda j, r: send(inb.at[1], 4, j, r, 2, 1).wait_send(), 0, half * steps - DIRECT)

    @pl.when(chip == 1)
    def _():
        pieces(
            lambda j, r: send(outb.at[1], 4, j, r, 2, 1).wait_send(),
            half * steps - DIRECT,
            half * steps,
        )


def state_copy(src, dst, send, recv, j, partner):
    return pltpu.make_async_remote_copy(
        src_ref=src.at[j],
        dst_ref=dst.at[j],
        send_sem=send.at[j],
        recv_sem=recv.at[j],
        device_id={"ctx": partner},
        device_id_type=MESH,
    )


def body(inputs, b_proj, c_proj, log_decay, starts, counts, skip_gain, readout):
    tokens, width = inputs.shape[1:]
    ctxs, heads_axis = lax.axis_size("ctx"), lax.axis_size("head")
    tiles = width // LANES
    half = tiles // 2
    spans = tokens // SPAN
    steps = SPAN // ROWS_STEP
    vmem, smem = pl.BlockSpec(memory_space=pltpu.VMEM), pl.BlockSpec(memory_space=pltpu.SMEM)
    hbm = pl.BlockSpec(memory_space=pltpu.HBM)
    big = lambda n, dtype: pltpu.VMEM((n, SPAN, LANES), dtype)
    small = lambda n: pltpu.VMEM((n, 8, LANES), F32)
    sem = pltpu.SemaphoreType.DMA
    return pl.pallas_call(
        functools.partial(kernel, (ctxs, heads_axis, tokens, tiles)),
        out_shape=(
            jax.ShapeDtypeStruct(inputs.shape, BF16),
            jax.ShapeDtypeStruct((1, tokens), F32),
        ),
        in_specs=[smem, hbm, hbm, hbm, hbm, hbm, smem, hbm],
        out_specs=(pl.BlockSpec(memory_space=pltpu.HBM), vmem),
        scratch_shapes=[
            pltpu.VMEM((tiles, tokens, LANES), BF16),
            sem((tiles,)),
            pltpu.VMEM(inputs.shape, BF16),
            pltpu.VMEM(b_proj.shape, BF16),
            pltpu.VMEM(c_proj.shape, BF16),
            pltpu.VMEM(log_decay.shape, BF16),
            pltpu.VMEM(starts.shape, starts.dtype),
            pltpu.VMEM((tiles, LANES), BF16),
            sem((6,)),
            pltpu.VMEM((tiles, tokens, LANES), BF16),
            pltpu.VMEM((tokens, width), BF16),
            pltpu.VMEM((tiles, tokens, LANES), F32),
            pltpu.VMEM((tokens, LANES), F32),
            pltpu.VMEM((SPAN, tokens), BF16),
            big(tiles, F32),
            big(tiles, F32),
            small(tiles),
            small(tiles),
            big(half, BF16),
            big(half, BF16),
            pltpu.VMEM((2, 4, 8, LANES), F32),
            small(4),
            small(4),
            big(half, F32),
            big(half, F32),
            small(4),
            small(4),
            pltpu.VMEM((2, half, SPAN, LANES), BF16),
            pltpu.VMEM((2, 4, 8, LANES), F32),
            pltpu.VMEM((3, half, SPAN, LANES), BF16),
            pltpu.VMEM((3, 4, 8, LANES), F32),
            big(tiles, BF16),
            big(half, BF16),
            pltpu.VMEM((2, 2, 8, LANES), F32),
            small(2),
            pltpu.VMEM((tiles, tokens, LANES), F32),
            pltpu.VMEM((spans, SPAN, SPAN), BF16),
            pltpu.VMEM((tokens // SUB, SUB, LANES), F32),
            pltpu.VMEM((heads_axis, tokens // LANES, LANES), F32),
            pltpu.VMEM((tiles, LANES), F32),
            sem((half,)), sem((half,)), sem((2,)),
            sem((5, half, steps)), sem((2, half, steps)), sem((4,)), sem((2,)),
            sem((half, steps)), sem((half, steps)), sem((2,)),
            pltpu.SemaphoreType.REGULAR((ctxs // 2,)), pltpu.SemaphoreType.REGULAR,
            sem((heads_axis,)), sem((heads_axis,)),
        ],
        compiler_params=pltpu.CompilerParams(collective_id=0, has_side_effects=True),
        name="ssd",
    )(counts, inputs, b_proj, c_proj, log_decay, starts, skip_gain, readout.reshape(tiles, LANES))


def solution(mesh):
    placed = (
        P("rep", "ctx", "head"),
        P("rep", "ctx", "head"),
        P("rep", "ctx", "head"),
        P("rep", "head", "ctx"),
        P("rep", "ctx"),
        P("rep", "ctx"),
        P("head"),
        P("head"),
    )
    return jax.shard_map(
        body,
        mesh=mesh,
        in_specs=placed,
        out_specs=(P("rep", "ctx", "head"), P("rep", "ctx")),
        check_vma=False,
    )
```
